256 devices in a mesh: seq: 64 (over y_lo, z, x), tp: 4 (over y_hi, core).
Axes of the slice: x: 4, y: 4 (y_hi: 2, y_lo: 2; y = y_hi * 2 + y_lo), z: 8, core: 2. Of those that a mesh axis runs over, the one named last changes fastest.
Arguments:
- queries: bfloat16 [16384, 1024], P('seq', 'tp'), may hold values from -6 to 6
- keys: bfloat16 [16384, 1024], P('seq', 'tp'), may hold values from -6 to 6
- values: bfloat16 [16384, 1024], P('seq', 'tp'), may hold values from -6 to 6
- out_weight: bfloat16 [1024, 5120], P('tp'), may hold values from -0.375 to 0.375
- residual: bfloat16 [16384, 5120], P(('seq', 'tp')), may hold values from -3 to 3
- gate: float32 [5120], replicated, may hold values from 0.5 to 1.5
- block_mask: int32 [128, 128], replicated, may hold values from 0 to 1, as said below
Outputs:
- updated: bfloat16 [16384, 5120], P(('seq', 'tp'))
The draws below stay inside these ranges and needn't reach their ends.
Inputs may be any that keep to these rules, and one draw needn't show every extreme that they name: block_mask[i, j] is 1 wherever |i - j| <= 4. Group the blocks by index of seq, 2 consecutive blocks to an index; where two indices lie more than 2 apart, the rows of one index's query blocks name at most one key block of the other index, and for indices exactly 3 apart this most is always reached.
All inputs are finite; a program needn't handle non-finite values.
Results may differ from the reference program's by a relative error of at most 0.012.
Values may be sent and summed in bfloat16 or wider, within the bound.
A program may use at most 128 MiB of HBM per device.

```python
import jax
import jax.numpy as jnp
from jax import lax

D = 5120
HD = 128
HEADS = 8
BLOCK = 128
BLK_DEV = 2
TOKENS = 16384
NB = 128


def paired_draw(key):
    base = jax.random.fold_in(key, 11)
    key_one, key_two = jax.random.split(base, 2)
    width = HEADS * HD
    query_field = 1.4 * jax.random.normal(key_one, (TOKENS, width), jnp.float32)
    key_field = 1.4 * jax.random.normal(key_two, (TOKENS, width), jnp.float32)
    query_field = jnp.clip(query_field, -6.0, 6.0)
    key_field = jnp.clip(key_field, -6.0, 6.0)
    return (query_field, key_field)


def draw_queries(key, part):
    return paired_draw(key)[0].astype(jnp.bfloat16)


def draw_keys(key, part):
    return paired_draw(key)[1].astype(jnp.bfloat16)


def draw_block_mask(key, part):
    per_device = BLK_DEV
    reach = (per_device + 3) // per_device
    device_count = NB // per_device
    rows = jnp.arange(NB, dtype=jnp.int32)[:, None]
    cols = jnp.arange(NB, dtype=jnp.int32)[None, :]
    distance = jnp.abs(rows - cols)
    ticket = jax.random.randint(jax.random.fold_in(key, 5), (NB, NB), 0, 4096)
    lucky = ticket * distance < 16384
    row_device = rows // per_device
    col_device = cols // per_device
    device_gap = jnp.abs(row_device - col_device)
    chosen = jax.random.randint(jax.random.fold_in(key, 7), (device_count, device_count), 0, per_device)
    chosen_here = chosen[row_device, col_device]
    near_keep = (distance <= 4) | lucky
    far_keep = (cols % per_device == chosen_here) & (lucky | (device_gap == reach + 1))
    keep = jnp.where(device_gap <= reach, near_keep, far_keep)
    return keep.astype(jnp.int32)


def levels(key, shape, cuts, low, largest):
    gain = 1.0
    for axis_at, shards_of in cuts:
        heights = jax.random.uniform(jax.random.fold_in(jax.random.fold_in(key, 6), axis_at), (shards_of,), jnp.float32, low / len(cuts), largest / len(cuts))
        gain = gain * jnp.repeat(jnp.exp(heights), shape[axis_at] // shards_of).reshape((-1,) + (1,) * (len(shape) - 1 - axis_at))
    return gain


def bell_draw(key, dims, scale, bound, shards=(), kind=jnp.bfloat16):
    entries = scale * jax.random.normal(key, dims, jnp.float32)
    if shards:
        entries = entries * levels(key, dims, shards, -0.22, 0.18)
    return jnp.clip(entries, -bound, bound).astype(kind)


def setup_inputs(seed: int = 0) -> dict:
    key_of = jax.random.split(jax.random.key(seed), 8)
    return {
        "queries": draw_queries(jax.random.fold_in(key_of[7], 71), 0),
        "keys": draw_keys(jax.random.fold_in(key_of[7], 71), 0),
        "values": bell_draw(key_of[2], (TOKENS, HEADS * HD), 1.0, 6.0, ((0, 64), (1, 4))),
        "out_weight": bell_draw(key_of[3], (HEADS * HD, D), (HD * 2) ** -0.5, 0.375, ((0, 4),)),
        "residual": bell_draw(key_of[4], (TOKENS, D), 0.5, 3.0, ((0, 256),)),
        "gate": jnp.clip(jax.random.uniform(key_of[5], (D,), jnp.float32, 0.5, 1.5), 0.5, 1.5),
        "block_mask": draw_block_mask(jax.random.fold_in(key_of[7], 71), 0),
    }


NEGATIVE = -1.0e30


def reference(queries, keys, values, out_weight, residual, gate, block_mask):
    score_scale = 1.0 / (HD ** 0.5)
    query_blocks = queries.reshape(NB, BLOCK, HEADS, HD)
    key_heads = keys.reshape(TOKENS, HEADS, HD).astype(jnp.float32)
    value_heads = values.reshape(TOKENS, HEADS, HD).astype(jnp.float32)

    def one_block(inputs):
        query_rows, mask_row = inputs
        scores = jnp.einsum("qhd,khd->hqk", query_rows.astype(jnp.float32), key_heads) * score_scale
        allowed = (jnp.repeat(mask_row, BLOCK) > 0)[None, None, :]
        scores = jnp.where(allowed, scores, NEGATIVE)
        row_top = jnp.max(scores, axis=-1, keepdims=True)
        weights = jnp.where(allowed, jnp.exp(scores - row_top), 0.0)
        totals = jnp.sum(weights, axis=-1)
        rounded = weights.astype(jnp.bfloat16).astype(jnp.float32)
        summed = jnp.einsum("hqk,khd->qhd", rounded, value_heads)
        return (summed / jnp.transpose(totals)[:, :, None]).astype(jnp.bfloat16)

    attended = lax.map(one_block, (query_blocks, block_mask)).reshape(TOKENS, HEADS * HD)
    branch = jnp.dot(attended, out_weight, preferred_element_type=jnp.float32)
    return (residual.astype(jnp.float32) + gate[None, :] * branch).astype(jnp.bfloat16)
```

```python
import functools

import jax
import jax.numpy as jnp
from jax import lax
from jax.experimental import pallas as pl
from jax.experimental.pallas import tpu as pltpu
from jax.sharding import PartitionSpec as P

HD = 128
BLOCK = 128
LOW = -1e30
BIG = 1e30
EXP2_SCALE = 1.4426950408889634 / HD**0.5
MESH = pl.DeviceIdType.MESH

NX = 4
NZ = 8
HALF = NX * NZ


def wait_bytes(ref, sem):
    pltpu.make_async_copy(ref, ref, sem).wait()


def attention_kernel(
    q_ref, k_ref, v_ref, mask_ref, att_ref,
    mask_s, qin, kv, acc, top, tot, o_send, o_recv, s_send, s_recv, att_send, att_buf,
    mask_sem, a_send, a_recv, q_send, q_recv, ring_send, ring_recv, sib_send,
    os_send, os_recv, d_send, d_recv,
):
    s = lax.axis_index("seq")
    t = lax.axis_index("tp")
    y_lo = s // HALF
    z = (s // NX) % NZ
    x = s % NX
    y_hi = t // 2
    c = t % 2
    plane = y_lo * HALF + z * NX
    z_up = y_lo * HALF + ((z + 1) % NZ) * NX + x
    z_down = y_lo * HALF + ((z + NZ - 1) % NZ) * NX + x
    partner = (1 - y_lo) * HALF + z * NX + x

    barrier = pltpu.get_barrier_semaphore()
    member = y_hi * 8 + x * 2 + c

    def greet(o, carry):
        m = (member + o) % 16
        pl.semaphore_signal(
            barrier, inc=1, device_id=(plane + (m // 2) % 4, (m // 8) * 2 + m % 2), device_id_type=MESH
        )
        return carry

    lax.fori_loop(1, 16, greet, 0)
    for other in (z_up, z_down, partner):
        pl.semaphore_signal(barrier, inc=1, device_id=(other, t), device_id_type=MESH)

    mask_copies = []
    for n, half in enumerate((y_lo, 1 - y_lo)):
        rows = pl.ds(pl.multiple_of((half * NZ + z) * 8, 8), 8)
        copy = pltpu.make_async_copy(mask_ref.at[rows], mask_s.at[n], mask_sem.at[n])
        copy.start()
        mask_copies.append(copy)
    top[...] = jnp.full(top.shape, LOW, jnp.float32)
    tot[...] = jnp.zeros(tot.shape, jnp.float32)
    acc[...] = jnp.zeros(acc.shape, jnp.float32)
    pl.semaphore_wait(barrier, 18)

    my_slot = z * NX + x
    for jj in range(2):
        j = 2 * c + jj
        columns = pl.ds(jj * HD, HD)
        pieces = ((k_ref, kv.at[my_slot, 0]), (v_ref, kv.at[my_slot, 1]), (q_ref, qin.at[x % 2]))
        for n, (src, dst) in enumerate(pieces):
            @pl.when(j != x)
            def _():
                pltpu.make_async_remote_copy(
                    src.at[:, columns], dst, a_send.at[jj, n], a_recv.at[x % 2, n],
                    device_id=(plane + j, y_hi * 2 + x // 2), device_id_type=MESH,
                ).start()

            @pl.when(j == x)
            def _():
                pltpu.make_async_copy(src.at[:, columns], dst, a_recv.at[x % 2, n]).start()

    def ring(idx, direction):
        pltpu.make_async_remote_copy(
            kv.at[idx], kv.at[idx], ring_send.at[direction, idx], ring_recv.at[idx],
            device_id=(z_up if direction == 0 else z_down, t), device_id_type=MESH,
        ).start()

    def to_sibling(idx):
        pltpu.make_async_remote_copy(
            kv.at[idx], kv.at[idx], sib_send.at[idx], ring_recv.at[idx],
            device_id=(s, y_hi * 2 + 1 - c), device_id_type=MESH,
        ).start()

    for e in range(2):
        idx = z * NX + 2 * c + e
        for n in range(2):
            wait_bytes(kv.at[idx, n], a_recv.at[e, n])
        ring(idx, 0)
        ring(idx, 1)
        to_sibling(idx)
    for i in range(2):
        wait_bytes(qin.at[i], a_recv.at[i, 2])
        pltpu.make_async_remote_copy(
            qin.at[i], qin.at[2 + i], q_send.at[i], q_recv.at[i],
            device_id=(partner, t), device_id_type=MESH,
        ).start()
    for copy in mask_copies:
        copy.wait()
    for i in range(2):
        wait_bytes(qin.at[2 + i], q_recv.at[i])

    lane = lax.broadcasted_iota(jnp.int32, (1, 2 * BLOCK), 1)

    def compute(zz, cc):
        b0 = zz * NX + 2 * cc
        g0 = y_lo * HALF + b0
        near = jnp.int32(0)
        for grp, half in enumerate((y_lo, 1 - y_lo)):
            for i in range(2):
                a = half * HALF + z * NX + 2 * c + i
                for e in range(2):
                    gap = a - (g0 + e)
                    near = near | ((gap <= 2) & (gap >= -2)).astype(jnp.int32)

        def one_round(rr, carry):
            for q in range(4):
                grp, i = q // 2, q % 2
                row = (2 * c + i) * 2
                halves_k, halves_v, conds = [], [], []
                for e in range(2):
                    col = 2 * (g0 + e)
                    m00 = mask_s[grp, row, col]
                    m10 = mask_s[grp, row + 1, col]
                    m01 = mask_s[grp, row, col + 1]
                    m11 = mask_s[grp, row + 1, col + 1]
                    block = (m01 | m11) ^ rr
                    upper = block != 0
                    allow0 = jnp.where(upper, m01, m00)
                    allow1 = jnp.where(upper, m11, m10)
                    conds.append(jnp.where(lane < BLOCK, allow0, allow1) != 0)
                    halves_k.append(jnp.where(upper, kv[b0 + e, 0, BLOCK:, :], kv[b0 + e, 0, :BLOCK, :]))
                    halves_v.append(jnp.where(upper, kv[b0 + e, 1, BLOCK:, :], kv[b0 + e, 1, :BLOCK, :]))
                kk = jnp.concatenate(halves_k, axis=0)
                vv = jnp.concatenate(halves_v, axis=0)
                scores = lax.dot_general(
                    kk, qin[q], (((1,), (1,)), ((), ())), preferred_element_type=jnp.float32
                )
                parts = (scores[:BLOCK], scores[BLOCK:])
                old = top[q]
                new = old
                for part, cond in zip(parts, conds):
                    new = jnp.maximum(new, jnp.where(cond, jnp.max(part, axis=0, keepdims=True), LOW))
                alpha = jnp.exp2((old - new) * EXP2_SCALE)
                scaled = new * EXP2_SCALE
                total = tot[q] * alpha
                weights = []
                for part, cond in zip(parts, conds):
                    weight = jnp.exp2(part * EXP2_SCALE - jnp.where(cond, scaled, BIG))
                    total = total + jnp.sum(weight, axis=0, keepdims=True)
                    weights.append(weight.astype(jnp.bfloat16))
                top[q] = new
                tot[q] = total
                added = lax.dot_general(
                    vv, jnp.concatenate(weights, axis=0), (((0,), (0,)), ((), ())),
                    preferred_element_type=jnp.float32,
                )
                acc[q] = acc[q] * alpha + added
            return carry

        lax.fori_loop(0, 1 + near, one_round, 0)

    def step(h, carry):
        u = h // 2
        e = h % 2
        r = (u + 1) // 2
        up = (u % 2 == 1).astype(jnp.int32)
        zz = (z + NZ + jnp.where(up == 1, -r, r)) % NZ
        idx = zz * NX + 2 * c + e

        @pl.when(u > 0)
        def _():
            wait_bytes(kv.at[idx], ring_recv.at[idx])
            to_sibling(idx)

            @pl.when((up == 1) & (r < 4 - e))
            def _():
                ring(idx, 0)

            @pl.when((up == 0) & (r < 3 + e))
            def _():
                ring(idx, 1)

        @pl.when(h > 0)
        def _():
            pu = jnp.where(e == 0, u - 1, u)
            pr = (pu + 1) // 2
            pz = (z + NZ + jnp.where(pu % 2 == 1, -pr, pr)) % NZ
            pc = jnp.where(e == 0, 1 - c, c)

            @pl.when(e == 0)
            def _():
                for n in range(2):
                    slot = pz * NX + 2 * pc + n
                    wait_bytes(kv.at[slot], ring_recv.at[slot])

            compute(pz, pc)

        return carry

    lax.fori_loop(0, 16, step, 0)
    last = (z + 4) % NZ
    for n in range(2):
        slot = last * NX + 2 * (1 - c) + n
        wait_bytes(kv.at[slot], ring_recv.at[slot])
    compute(last, 1 - c)

    for i in range(2):
        o_send[i] = acc[2 + i].astype(jnp.bfloat16)
        s_send[pl.ds(2 * i, 1), :] = top[2 + i]
        s_send[pl.ds(2 * i + 1, 1), :] = tot[2 + i]
    partial = []
    for n, (src, dst) in enumerate(((s_send, s_recv), (o_send, o_recv))):
        copy = pltpu.make_async_remote_copy(
            src, dst, os_send.at[n], os_recv.at[n], device_id=(partner, t), device_id_type=MESH
        )
        copy.start()
        partial.append(copy)
    for copy in partial:
        copy.wait_recv()
    for i in range(2):
        top_one, tot_one = top[i], tot[i]
        top_two, tot_two = s_recv[pl.ds(2 * i, 1), :], s_recv[pl.ds(2 * i + 1, 1), :]
        both = jnp.maximum(top_one, top_two)
        one = jnp.exp2((top_one - both) * EXP2_SCALE)
        two = jnp.exp2((top_two - both) * EXP2_SCALE)
        total = tot_one * one + tot_two * two
        merged = (acc[i] * one + o_recv[i].astype(jnp.float32) * two) / total
        att_send[i] = merged.T.astype(jnp.bfloat16)

    head = y_hi * NX + x
    rows = att_buf.shape[1]
    for i in range(2):
        for other in range(4):
            src = att_send.at[i, pl.ds(other * rows, rows)]
            mine = (2 * c + i == x) & (t == other)

            @pl.when(jnp.logical_not(mine))
            def _():
                pltpu.make_async_remote_copy(
                    src, att_buf.at[head], d_send.at[i, other], d_recv.at[head],
                    device_id=(plane + 2 * c + i, other), device_id_type=MESH,
                ).start()

            @pl.when(mine)
            def _():
                pltpu.make_async_copy(src, att_buf.at[head], d_recv.at[head]).start()

    for h in range(8):
        wait_bytes(att_buf.at[h], d_recv.at[h])
    att_ref[...] = att_buf[...]

    for jj in range(2):
        @pl.when(2 * c + jj != x)
        def _():
            for n in range(3):
                wait_bytes(qin.at[0], a_send.at[jj, n])
    for i in range(2):
        wait_bytes(qin.at[i], q_send.at[i])
    for copy in partial:
        copy.wait_send()
    for i in range(2):
        for other in range(4):
            @pl.when(jnp.logical_not((2 * c + i == x) & (t == other)))
            def _():
                wait_bytes(att_buf.at[0], d_send.at[i, other])

    def drain(h, carry):
        u = h // 2
        e = h % 2
        r = (u + 1) // 2
        up = (u % 2 == 1).astype(jnp.int32)
        zz = (z + NZ + jnp.where(up == 1, -r, r)) % NZ
        idx = zz * NX + 2 * c + e
        wait_bytes(kv.at[idx], sib_send.at[idx])

        @pl.when((u == 0) | ((up == 1) & (r < 4 - e)))
        def _():
            wait_bytes(kv.at[idx], ring_send.at[0, idx])

        @pl.when((u == 0) | ((up == 0) & (r < 3 + e)))
        def _():
            wait_bytes(kv.at[idx], ring_send.at[1, idx])

        return carry

    lax.fori_loop(0, 16, drain, 0)


def shards(queries, keys, values, out_weight, residual, gate, block_mask):
    rows = residual.shape[0]
    toks = queries.shape[0]
    bf16, f32 = jnp.bfloat16, jnp.float32
    dma = pltpu.SemaphoreType.DMA
    att = pl.pallas_call(
        attention_kernel,
        out_shape=jax.ShapeDtypeStruct((8, rows, HD), bf16),
        in_specs=[pl.BlockSpec(memory_space=pl.ANY)] * 4,
        out_specs=pl.BlockSpec(memory_space=pltpu.VMEM),
        scratch_shapes=[
            pltpu.SMEM((2, 8, 128), jnp.int32),
            pltpu.VMEM((4, toks, HD), bf16),
            pltpu.VMEM((HALF, 2, toks, HD), bf16),
            pltpu.VMEM((4, HD, toks), f32),
            pltpu.VMEM((4, 1, toks), f32),
            pltpu.VMEM((4, 1, toks), f32),
            pltpu.VMEM((2, HD, toks), bf16),
            pltpu.VMEM((2, HD, toks), bf16),
            pltpu.VMEM((8, toks), f32),
            pltpu.VMEM((8, toks), f32),
            pltpu.VMEM((2, toks, HD), bf16),
            pltpu.VMEM((8, rows, HD), bf16),
            dma((2,)), dma((2, 3)), dma((2, 3)), dma((2,)), dma((2,)),
            dma((2, HALF)), dma((HALF,)), dma((HALF,)),
            dma((2,)), dma((2,)), dma((2, 4)), dma((8,)),
        ],
        compiler_params=pltpu.CompilerParams(
            collective_id=0, has_side_effects=True, vmem_limit_bytes=32 * 1024 * 1024
        ),
        name="attend",
    )(queries, keys, values, block_mask)
    att = jnp.transpose(att, (1, 0, 2)).reshape(rows, 8 * HD)
    weight = lax.all_gather(out_weight, "tp", axis=0, tiled=True)
    branch = jnp.dot(att, weight, preferred_element_type=f32)
    return (residual.astype(f32) + gate[None, :] * branch).astype(bf16)


def solution(mesh):
    return jax.shard_map(
        shards,
        mesh=mesh,
        in_specs=(
            P("seq", "tp"),
            P("seq", "tp"),
            P("seq", "tp"),
            P("tp", None),
            P(("seq", "tp"), None),
            P(),
            P(),
        ),
        out_specs=P(("seq", "tp"), None),
        check_vma=False,
    )
```

```python
import functools

import jax
import jax.numpy as jnp
from jax import lax
from jax.experimental import pallas as pl
from jax.experimental.pallas import tpu as pltpu
from jax.sharding import PartitionSpec as P

HD = 128
BLOCK = 128
LOW = -1e30
BIG = 1e30
EXP2_SCALE = 1.4426950408889634 / HD**0.5
MESH = pl.DeviceIdType.MESH

NX = 4
NZ = 8
HALF = NX * NZ


W_PLAN = (
    (2, 0, 1), (4, 1, 0), (5, 0, 2), (7, 1, 1), (8, 0, 3), (10, 1, 2), (11, 2, 0), (12, 2, 1), (13, 1, 3),
)


def wait_bytes(ref, sem):
    pltpu.make_async_copy(ref, ref, sem).wait()


def attention_kernel(
    q_ref, k_ref, v_ref, w_ref, res_ref, gate_ref, mask_ref, out_ref,
    mask_s, qin, kv, acc, top, tot, o_send, o_recv, s_send, s_recv, att_send, att_buf,
    wbuf, res, gate, branch,
    mask_sem, a_send, a_recv, q_send, q_recv, ring_send, ring_recv, sib_send,
    os_send, os_recv, d_send, d_recv,
    local_sem, cross_send, w_recv, x_send, wsib_send, wsib_recv, own_send, own_recv,
):
    s = lax.axis_index("seq")
    t = lax.axis_index("tp")
    y_lo = s // HALF
    z = (s // NX) % NZ
    x = s % NX
    y_hi = t // 2
    c = t % 2
    plane = y_lo * HALF + z * NX
    z_up = y_lo * HALF + ((z + 1) % NZ) * NX + x
    z_down = y_lo * HALF + ((z + NZ - 1) % NZ) * NX + x
    partner = (1 - y_lo) * HALF + z * NX + x
    x_up = plane + (x + 1) % NX
    x_down = plane + (x + NX - 1) % NX
    sibling = y_hi * 2 + 1 - c
    facing = (1 - y_hi) * 2 + c

    barrier = pltpu.get_barrier_semaphore()
    member = y_hi * 8 + x * 2 + c

    def greet(o, carry):
        m = (member + o) % 16
        pl.semaphore_signal(
            barrier, inc=1, device_id=(plane + (m // 2) % 4, (m // 8) * 2 + m % 2), device_id_type=MESH
        )
        return carry

    lax.fori_loop(1, 16, greet, 0)
    for other in (z_up, z_down, partner):
        pl.semaphore_signal(barrier, inc=1, device_id=(other, t), device_id_type=MESH)
    pl.semaphore_signal(barrier, inc=1, device_id=(partner, facing), device_id_type=MESH)

    mask_copies = []
    for n, half in enumerate((y_lo, 1 - y_lo)):
        rows = pl.ds(pl.multiple_of((half * NZ + z) * 8, 8), 8)
        copy = pltpu.make_async_copy(mask_ref.at[rows], mask_s.at[n], mask_sem.at[n])
        copy.start()
        mask_copies.append(copy)
    top[...] = jnp.full(top.shape, LOW, jnp.float32)
    tot[...] = jnp.zeros(tot.shape, jnp.float32)
    acc[...] = jnp.zeros(acc.shape, jnp.float32)
    local = []
    for n, (src, dst) in enumerate(((w_ref, wbuf.at[t]), (res_ref, res), (gate_ref, gate))):
        copy = pltpu.make_async_copy(src, dst, local_sem.at[n])
        copy.start()
        local.append(copy)
    pl.semaphore_wait(barrier, 19)

    my_slot = z * NX + x
    pieces = ((k_ref, kv.at[my_slot, 0]), (v_ref, kv.at[my_slot, 1]), (q_ref, qin.at[x % 2]))
    for jj, n in ((0, 0), (1, 0), (0, 1), (1, 1), (0, 2), (1, 2)):
        j = 2 * c + jj
        src, dst = pieces[n]
        columns = pl.ds(jj * HD, HD)

        @pl.when(j != x)
        def _():
            pltpu.make_async_remote_copy(
                src.at[:, columns], dst, a_send.at[jj, n], a_recv.at[x % 2, n],
                device_id=(plane + j, y_hi * 2 + x // 2), device_id_type=MESH,
            ).start()

        @pl.when(j == x)
        def _():
            pltpu.make_async_copy(src.at[:, columns], dst, a_recv.at[x % 2, n]).start()

    quarter = w_ref.shape[0] // NX
    chunk = quarter // 4

    def chunk_rows(qx, m):
        return pl.ds(pl.multiple_of(qx * quarter + m * chunk, 8), chunk)

    for m in range(4):
        pltpu.make_async_remote_copy(
            w_ref.at[chunk_rows(x, m)], wbuf.at[t, chunk_rows(x, m)], cross_send.at[m], w_recv.at[x * 4 + m],
            device_id=(partner, facing), device_id_type=MESH,
        ).start()

    def w_piece(qx, m):
        return wbuf.at[facing, chunk_rows(qx, m)]

    def w_to(qx, m, direction):
        piece = w_piece(qx, m)
        pltpu.make_async_remote_copy(
            piece, piece, x_send.at[direction, qx * 4 + m], w_recv.at[qx * 4 + m],
            device_id=(x_up if direction == 0 else x_down, t), device_id_type=MESH,
        ).start()

    def w_sibling(qx, m):
        piece = w_piece(qx, m)
        pltpu.make_async_remote_copy(
            piece, piece, wsib_send, wsib_recv, device_id=(s, sibling), device_id_type=MESH
        ).start()

    def w_first(m):
        wait_bytes(w_piece(x, m), w_recv.at[x * 4 + m])
        w_to(x, m, 0)
        w_to(x, m, 1)
        w_sibling(x, m)

    def w_second(m):
        below, above = (x + NX - 1) % NX, (x + 1) % NX
        wait_bytes(w_piece(below, m), w_recv.at[below * 4 + m])
        if m % 2 == 0:
            w_to(below, m, 0)
        w_sibling(below, m)
        wait_bytes(w_piece(above, m), w_recv.at[above * 4 + m])
        if m % 2 == 1:
            w_to(above, m, 1)
        w_sibling(above, m)

    def w_third(m):
        far = (x + 2) % NX
        wait_bytes(w_piece(far, m), w_recv.at[far * 4 + m])
        w_sibling(far, m)

    def ring(idx, direction):
        pltpu.make_async_remote_copy(
            kv.at[idx], kv.at[idx], ring_send.at[direction, idx], ring_recv.at[idx],
            device_id=(z_up if direction == 0 else z_down, t), device_id_type=MESH,
        ).start()

    def to_sibling(idx):
        pltpu.make_async_remote_copy(
            kv.at[idx], kv.at[idx], sib_send.at[idx], ring_recv.at[idx],
            device_id=(s, sibling), device_id_type=MESH,
        ).start()

    for e in range(2):
        idx = z * NX + 2 * c + e
        for n in range(2):
            wait_bytes(kv.at[idx, n], a_recv.at[e, n])
        ring(idx, 0)
        ring(idx, 1)
        to_sibling(idx)
    for i in range(2):
        wait_bytes(qin.at[i], a_recv.at[i, 2])
        pltpu.make_async_remote_copy(
            qin.at[i], qin.at[2 + i], q_send.at[i], q_recv.at[i],
            device_id=(partner, t), device_id_type=MESH,
        ).start()
    for copy in mask_copies:
        copy.wait()
    w_first(0)

    lane = lax.broadcasted_iota(jnp.int32, (1, 2 * BLOCK), 1)

    def compute(zz, cc):
        b0 = zz * NX + 2 * cc
        g0 = y_lo * HALF + b0
        near = jnp.int32(0)
        for grp, half in enumerate((y_lo, 1 - y_lo)):
            for i in range(2):
                a = half * HALF + z * NX + 2 * c + i
                for e in range(2):
                    gap = a - (g0 + e)
                    near = near | ((gap <= 2) & (gap >= -2)).astype(jnp.int32)

        def one_round(rr, carry):
            for q in range(4):
                grp, i = q // 2, q % 2
                row = (2 * c + i) * 2
                halves_k, halves_v, conds = [], [], []
                for e in range(2):
                    col = 2 * (g0 + e)
                    m00 = mask_s[grp, row, col]
                    m10 = mask_s[grp, row + 1, col]
                    m01 = mask_s[grp, row, col + 1]
                    m11 = mask_s[grp, row + 1, col + 1]
                    block = (m01 | m11) ^ rr
                    upper = block != 0
                    allow0 = jnp.where(upper, m01, m00)
                    allow1 = jnp.where(upper, m11, m10)
                    conds.append(jnp.where(lane < BLOCK, allow0, allow1) != 0)
                    halves_k.append(jnp.where(upper, kv[b0 + e, 0, BLOCK:, :], kv[b0 + e, 0, :BLOCK, :]))
                    halves_v.append(jnp.where(upper, kv[b0 + e, 1, BLOCK:, :], kv[b0 + e, 1, :BLOCK, :]))
                kk = jnp.concatenate(halves_k, axis=0)
                vv = jnp.concatenate(halves_v, axis=0)
                scores = lax.dot_general(
                    kk, qin[q], (((1,), (1,)), ((), ())), preferred_element_type=jnp.float32
                )
                parts = (scores[:BLOCK], scores[BLOCK:])
                old = top[q]
                new = old
                for part, cond in zip(parts, conds):
                    new = jnp.maximum(new, jnp.where(cond, jnp.max(part, axis=0, keepdims=True), LOW))
                alpha = jnp.exp2((old - new) * EXP2_SCALE)
                scaled = new * EXP2_SCALE
                total = tot[q] * alpha
                weights = []
                for part, cond in zip(parts, conds):
                    weight = jnp.exp2(part * EXP2_SCALE - jnp.where(cond, scaled, BIG))
                    total = total + jnp.sum(weight, axis=0, keepdims=True)
                    weights.append(weight.astype(jnp.bfloat16))
                top[q] = new
                tot[q] = total
                added = lax.dot_general(
                    vv, jnp.concatenate(weights, axis=0), (((0,), (0,)), ((), ())),
                    preferred_element_type=jnp.float32,
                )
                acc[q] = acc[q] * alpha + added
            return carry

        lax.fori_loop(0, 1 + near, one_round, 0)

    def step(h, carry):
        u = h // 2
        e = h % 2
        r = (u + 1) // 2
        up = (u % 2 == 1).astype(jnp.int32)
        zz = (z + NZ + jnp.where(up == 1, -r, r)) % NZ
        idx = zz * NX + 2 * c + e

        @pl.when(u > 0)
        def _():
            wait_bytes(kv.at[idx], ring_recv.at[idx])
            to_sibling(idx)

            @pl.when((up == 1) & (r < 4 - e))
            def _():
                ring(idx, 0)

            @pl.when((up == 0) & (r < 3 + e))
            def _():
                ring(idx, 1)

        own_rows = pl.ds(pl.multiple_of(h * chunk, 8), chunk)
        pltpu.make_async_remote_copy(
            w_ref.at[own_rows], wbuf.at[t, own_rows], own_send, own_recv,
            device_id=(s, sibling), device_id_type=MESH,
        ).start()

        for at, event, m in W_PLAN:
            @pl.when(h == at)
            def _():
                (w_first, w_second, w_third)[event](m)

        @pl.when(h == 1)
        def _():
            for i in range(2):
                wait_bytes(qin.at[2 + i], q_recv.at[i])

        @pl.when(h > 0)
        def _():
            pu = jnp.where(e == 0, u - 1, u)
            pr = (pu + 1) // 2
            pz = (z + NZ + jnp.where(pu % 2 == 1, -pr, pr)) % NZ
            pc = jnp.where(e == 0, 1 - c, c)

            @pl.when(e == 0)
            def _():
                for n in range(2):
                    slot = pz * NX + 2 * pc + n
                    wait_bytes(kv.at[slot], ring_recv.at[slot])

            compute(pz, pc)

        return carry

    lax.fori_loop(0, 16, step, 0)
    last = (z + 4) % NZ
    for n in range(2):
        slot = last * NX + 2 * (1 - c) + n
        wait_bytes(kv.at[slot], ring_recv.at[slot])
    compute(last, 1 - c)

    w_third(2)
    w_third(3)

    partial = []
    for i in range(2):
        o_send[i] = acc[2 + i].astype(jnp.bfloat16)
        s_send[i, pl.ds(0, 1), :] = top[2 + i]
        s_send[i, pl.ds(1, 1), :] = tot[2 + i]
        for n, (src, dst) in enumerate(((s_send, s_recv), (o_send, o_recv))):
            copy = pltpu.make_async_remote_copy(
                src.at[i], dst.at[i], os_send.at[i, n], os_recv.at[i, n],
                device_id=(partner, t), device_id_type=MESH,
            )
            copy.start()
            partial.append(copy)
    head = y_hi * NX + x
    rows = att_buf.shape[1]
    for i in range(2):
        partial[2 * i].wait_recv()
        partial[2 * i + 1].wait_recv()
        top_one, tot_one = top[i], tot[i]
        top_two, tot_two = s_recv[i, pl.ds(0, 1), :], s_recv[i, pl.ds(1, 1), :]
        both = jnp.maximum(top_one, top_two)
        one = jnp.exp2((top_one - both) * EXP2_SCALE)
        two = jnp.exp2((top_two - both) * EXP2_SCALE)
        total = tot_one * one + tot_two * two
        merged = (acc[i] * one + o_recv[i].astype(jnp.float32) * two) / total
        att_send[i] = merged.T.astype(jnp.bfloat16)
        for other in range(4):
            src = att_send.at[i, pl.ds(other * rows, rows)]
            mine = (2 * c + i == x) & (t == other)

            @pl.when(jnp.logical_not(mine))
            def _():
                pltpu.make_async_remote_copy(
                    src, att_buf.at[head], d_send.at[i, other], d_recv.at[head],
                    device_id=(plane + 2 * c + i, other), device_id_type=MESH,
                ).start()

            @pl.when(mine)
            def _():
                pltpu.make_async_copy(src, att_buf.at[head], d_recv.at[head]).start()

    for copy in local:
        copy.wait()
    wait_bytes(wbuf.at[y_hi * 2 + 1 - c], own_recv)
    width = 512

    def project(base, columns):
        total = None
        for n in range(2):
            pair = jnp.concatenate([att_buf[base * 4 + 2 * n], att_buf[base * 4 + 2 * n + 1]], axis=1)
            term = jnp.dot(pair, wbuf[base * 2 + n, :, columns], preferred_element_type=jnp.float32)
            total = term if total is None else total + term
        return total

    for n in range(NX):
        h = y_hi * NX + n
        wait_bytes(att_buf.at[h], d_recv.at[h])

    def first_half(n, carry):
        columns = pl.ds(pl.multiple_of(n * width, width), width)
        branch[:, columns] = project(y_hi, columns)
        return carry

    lax.fori_loop(0, out_ref.shape[1] // width, first_half, 0)
    for n in range(NX):
        h = (1 - y_hi) * NX + n
        wait_bytes(att_buf.at[h], d_recv.at[h])
    wait_bytes(wbuf.at[(1 - y_hi) * 2 + 1 - c], wsib_recv)

    def second_half(n, carry):
        columns = pl.ds(pl.multiple_of(n * width, width), width)
        total = branch[:, columns] + project(1 - y_hi, columns)
        out_ref[:, columns] = (
            res[:, columns].astype(jnp.float32) + gate[:, columns] * total
        ).astype(out_ref.dtype)
        return carry

    lax.fori_loop(0, out_ref.shape[1] // width, second_half, 0)

    for jj in range(2):
        @pl.when(2 * c + jj != x)
        def _():
            for n in range(3):
                wait_bytes(qin.at[0], a_send.at[jj, n])
    for i in range(2):
        wait_bytes(qin.at[i], q_send.at[i])
    for copy in partial:
        copy.wait_send()
    for i in range(2):
        for other in range(4):
            @pl.when(jnp.logical_not((2 * c + i == x) & (t == other)))
            def _():
                wait_bytes(att_buf.at[0], d_send.at[i, other])
    wait_bytes(wbuf.at[0], own_send)
    wait_bytes(wbuf.at[0], wsib_send)
    below, above = (x + NX - 1) % NX, (x + 1) % NX
    for m in range(4):
        wait_bytes(w_piece(x, m), cross_send.at[m])
        wait_bytes(w_piece(x, m), x_send.at[0, x * 4 + m])
        wait_bytes(w_piece(x, m), x_send.at[1, x * 4 + m])
        if m % 2 == 0:
            wait_bytes(w_piece(x, m), x_send.at[0, below * 4 + m])
        else:
            wait_bytes(w_piece(x, m), x_send.at[1, above * 4 + m])

    def drain(h, carry):
        u = h // 2
        e = h % 2
        r = (u + 1) // 2
        up = (u % 2 == 1).astype(jnp.int32)
        zz = (z + NZ + jnp.where(up == 1, -r, r)) % NZ
        idx = zz * NX + 2 * c + e
        wait_bytes(kv.at[idx], sib_send.at[idx])

        @pl.when((u == 0) | ((up == 1) & (r < 4 - e)))
        def _():
            wait_bytes(kv.at[idx], ring_send.at[0, idx])

        @pl.when((u == 0) | ((up == 0) & (r < 3 + e)))
        def _():
            wait_bytes(kv.at[idx], ring_send.at[1, idx])

        return carry

    lax.fori_loop(0, 16, drain, 0)


def shards(queries, keys, values, out_weight, residual, gate, block_mask):
    rows = residual.shape[0]
    toks = queries.shape[0]
    bf16, f32 = jnp.bfloat16, jnp.float32
    dma = pltpu.SemaphoreType.DMA
    width = residual.shape[1]
    return pl.pallas_call(
        attention_kernel,
        out_shape=jax.ShapeDtypeStruct((rows, width), bf16),
        in_specs=[pl.BlockSpec(memory_space=pl.ANY)] * 7,
        out_specs=pl.BlockSpec(memory_space=pltpu.VMEM),
        scratch_shapes=[
            pltpu.SMEM((2, 8, 128), jnp.int32),
            pltpu.VMEM((4, toks, HD), bf16),
            pltpu.VMEM((HALF, 2, toks, HD), bf16),
            pltpu.VMEM((4, HD, toks), f32),
            pltpu.VMEM((4, 1, toks), f32),
            pltpu.VMEM((4, 1, toks), f32),
            pltpu.VMEM((2, HD, toks), bf16),
            pltpu.VMEM((2, HD, toks), bf16),
            pltpu.VMEM((2, 8, toks), f32),
            pltpu.VMEM((2, 8, toks), f32),
            pltpu.VMEM((2, toks, HD), bf16),
            pltpu.VMEM((8, rows, HD), bf16),
            pltpu.VMEM((4, out_weight.shape[0], width), bf16),
            pltpu.VMEM((rows, width), bf16),
            pltpu.VMEM((1, width), f32),
            pltpu.VMEM((rows, width), f32),
            dma((2,)), dma((2, 3)), dma((2, 3)), dma((2,)), dma((2,)),
            dma((2, HALF)), dma((HALF,)), dma((HALF,)),
            dma((2, 2)), dma((2, 2)), dma((2, 4)), dma((8,)),
            dma((3,)), dma((4,)), dma((16,)), dma((2, 16)), dma, dma, dma, dma,
        ],
        compiler_params=pltpu.CompilerParams(collective_id=0, has_side_effects=True),
        name="attend",
    )(queries, keys, values, out_weight, residual, gate.reshape(1, width), block_mask)


def solution(mesh):
    return jax.shard_map(
        shards,
        mesh=mesh,
        in_specs=(
            P("seq", "tp"),
            P("seq", "tp"),
            P("seq", "tp"),
            P("tp", None),
            P(("seq", "tp"), None),
            P(),
            P(),
        ),
        out_specs=P(("seq", "tp"), None),
        check_vma=False,
    )
```

```python
import functools

import jax
import jax.numpy as jnp
from jax import lax
from jax.experimental import pallas as pl
from jax.experimental.pallas import tpu as pltpu
from jax.sharding import PartitionSpec as P

HD = 128
BLOCK = 128
LOW = -1e30
BIG = 1e30
EXP2_SCALE = 1.4426950408889634 / HD**0.5
MESH = pl.DeviceIdType.MESH

NX = 4
NZ = 8
HALF = NX * NZ


W_PLAN = (
    (0, 0, 1), (2, 1, 0), (3, 0, 2), (5, 1, 1), (6, 0, 3), (8, 1, 2), (9, 2, 0), (10, 2, 1), (11, 1, 3),
)


def wait_bytes(ref, sem):
    pltpu.make_async_copy(ref, ref, sem).wait()


def attention_kernel(
    q_ref, k_ref, v_ref, w_ref, res_ref, gate_ref, mask_ref, out_ref,
    mask_s, qin, kv, acc, top, tot, o_send, o_recv, s_send, s_recv, att_send, att_buf,
    wbuf, res, gate, branch, scores, weights, alphas,
    mask_sem, a_send, a_recv, q_send, q_recv, ring_send, ring_recv, sib_send,
    os_send, os_recv, d_send, d_recv,
    local_sem, cross_send, w_recv, x_send, wsib_send, wsib_recv, own_send, own_recv,
):
    s = lax.axis_index("seq")
    t = lax.axis_index("tp")
    y_lo = s // HALF
    z = (s // NX) % NZ
    x = s % NX
    y_hi = t // 2
    c = t % 2
    plane = y_lo * HALF + z * NX
    z_up = y_lo * HALF + ((z + 1) % NZ) * NX + x
    z_down = y_lo * HALF + ((z + NZ - 1) % NZ) * NX + x
    partner = (1 - y_lo) * HALF + z * NX + x
    x_up = plane + (x + 1) % NX
    x_down = plane + (x + NX - 1) % NX
    sibling = y_hi * 2 + 1 - c
    facing = (1 - y_hi) * 2 + c

    barrier = pltpu.get_barrier_semaphore()
    member = y_hi * 8 + x * 2 + c

    def greet(o, carry):
        m = (member + o) % 16
        pl.semaphore_signal(
            barrier, inc=1, device_id=(plane + (m // 2) % 4, (m // 8) * 2 + m % 2), device_id_type=MESH
        )
        return carry

    lax.fori_loop(1, 16, greet, 0)
    for other in (z_up, z_down, partner):
        pl.semaphore_signal(barrier, inc=1, device_id=(other, t), device_id_type=MESH)
    pl.semaphore_signal(barrier, inc=1, device_id=(partner, facing), device_id_type=MESH)

    mask_copies = []
    for n, half in enumerate((y_lo, 1 - y_lo)):
        rows = pl.ds(pl.multiple_of((half * NZ + z) * 8, 8), 8)
        copy = pltpu.make_async_copy(mask_ref.at[rows], mask_s.at[n], mask_sem.at[n])
        copy.start()
        mask_copies.append(copy)
    top[...] = jnp.full(top.shape, LOW, jnp.float32)
    tot[...] = jnp.zeros(tot.shape, jnp.float32)
    acc[...] = jnp.zeros(acc.shape, jnp.float32)
    local = []
    for n, (src, dst) in enumerate(((w_ref, wbuf.at[t]), (res_ref, res), (gate_ref, gate))):
        copy = pltpu.make_async_copy(src, dst, local_sem.at[n])
        copy.start()
        local.append(copy)
    pl.semaphore_wait(barrier, 19)

    my_slot = z * NX + x
    pieces = ((k_ref, kv.at[my_slot, 0]), (v_ref, kv.at[my_slot, 1]), (q_ref, qin.at[x % 2]))
    for jj, n in ((0, 0), (1, 0), (0, 1), (1, 1), (0, 2), (1, 2)):
        j = 2 * c + jj
        src, dst = pieces[n]
        columns = pl.ds(jj * HD, HD)

        @pl.when(j != x)
        def _():
            pltpu.make_async_remote_copy(
                src.at[:, columns], dst, a_send.at[jj, n], a_recv.at[x % 2, n],
                device_id=(plane + j, y_hi * 2 + x // 2), device_id_type=MESH,
            ).start()

        @pl.when(j == x)
        def _():
            pltpu.make_async_copy(src.at[:, columns], dst, a_recv.at[x % 2, n]).start()

    quarter = w_ref.shape[0] // NX
    chunk = quarter // 4

    def chunk_rows(qx, m):
        return pl.ds(pl.multiple_of(qx * quarter + m * chunk, 8), chunk)

    for m in range(4):
        pltpu.make_async_remote_copy(
            w_ref.at[chunk_rows(x, m)], wbuf.at[t, chunk_rows(x, m)], cross_send.at[m], w_recv.at[x * 4 + m],
            device_id=(partner, facing), device_id_type=MESH,
        ).start()

    def w_piece(qx, m):
        return wbuf.at[facing, chunk_rows(qx, m)]

    def w_to(qx, m, direction):
        piece = w_piece(qx, m)
        pltpu.make_async_remote_copy(
            piece, piece, x_send.at[direction, qx * 4 + m], w_recv.at[qx * 4 + m],
            device_id=(x_up if direction == 0 else x_down, t), device_id_type=MESH,
        ).start()

    def w_sibling(qx, m):
        piece = w_piece(qx, m)
        pltpu.make_async_remote_copy(
            piece, piece, wsib_send, wsib_recv, device_id=(s, sibling), device_id_type=MESH
        ).start()

    def w_first(m):
        wait_bytes(w_piece(x, m), w_recv.at[x * 4 + m])
        w_to(x, m, 0)
        w_to(x, m, 1)
        w_sibling(x, m)

    def w_second(m):
        below, above = (x + NX - 1) % NX, (x + 1) % NX
        wait_bytes(w_piece(below, m), w_recv.at[below * 4 + m])
        if m % 2 == 0:
            w_to(below, m, 0)
        w_sibling(below, m)
        wait_bytes(w_piece(above, m), w_recv.at[above * 4 + m])
        if m % 2 == 1:
            w_to(above, m, 1)
        w_sibling(above, m)

    def w_third(m):
        far = (x + 2) % NX
        wait_bytes(w_piece(far, m), w_recv.at[far * 4 + m])
        w_sibling(far, m)

    def ring(idx, direction):
        pltpu.make_async_remote_copy(
            kv.at[idx], kv.at[idx], ring_send.at[direction, idx], ring_recv.at[idx],
            device_id=(z_up if direction == 0 else z_down, t), device_id_type=MESH,
        ).start()

    def to_sibling(idx):
        pltpu.make_async_remote_copy(
            kv.at[idx], kv.at[idx], sib_send.at[idx], ring_recv.at[idx],
            device_id=(s, sibling), device_id_type=MESH,
        ).start()

    for n in range(2):
        for e in range(2):
            idx = z * NX + 2 * c + e
            piece = kv.at[idx, n]
            wait_bytes(piece, a_recv.at[e, n])
            for goal, sem in (
                ((z_up, t), ring_send.at[0, idx]), ((z_down, t), ring_send.at[1, idx]),
                ((s, sibling), sib_send.at[idx]),
            ):
                pltpu.make_async_remote_copy(
                    piece, piece, sem, ring_recv.at[idx], device_id=goal, device_id_type=MESH
                ).start()
    for i in range(2):
        wait_bytes(qin.at[i], a_recv.at[i, 2])
        pltpu.make_async_remote_copy(
            qin.at[i], qin.at[2 + i], q_send.at[i], q_recv.at[i],
            device_id=(partner, t), device_id_type=MESH,
        ).start()
    for copy in mask_copies:
        copy.wait()
    w_first(0)

    lane = lax.broadcasted_iota(jnp.int32, (1, 2 * BLOCK), 1)

    def compute(zz, cc):
        b0 = zz * NX + 2 * cc
        g0 = y_lo * HALF + b0
        near = jnp.int32(0)
        for grp, half in enumerate((y_lo, 1 - y_lo)):
            for i in range(2):
                a = half * HALF + z * NX + 2 * c + i
                for e in range(2):
                    gap = a - (g0 + e)
                    near = near | ((gap <= 2) & (gap >= -2)).astype(jnp.int32)

        def one_round(rr, carry):
            state = []
            for q in range(4):
                grp, i = q // 2, q % 2
                row = (2 * c + i) * 2
                halves_k, uppers, conds = [], [], []
                for e in range(2):
                    col = 2 * (g0 + e)
                    m00 = mask_s[grp, row, col]
                    m10 = mask_s[grp, row + 1, col]
                    m01 = mask_s[grp, row, col + 1]
                    m11 = mask_s[grp, row + 1, col + 1]
                    upper = ((m01 | m11) ^ rr) != 0
                    conds.append((jnp.where(upper, m01, m00), jnp.where(upper, m11, m10)))
                    uppers.append(upper)
                    halves_k.append(jnp.where(upper, kv[b0 + e, 0, BLOCK:, :], kv[b0 + e, 0, :BLOCK, :]))
                scores[q] = lax.dot_general(
                    jnp.concatenate(halves_k, axis=0), qin[q], (((1,), (1,)), ((), ())),
                    preferred_element_type=jnp.float32,
                )
                state.append((uppers, [jnp.where(lane < BLOCK, *pair) != 0 for pair in conds]))
            for q in range(4):
                uppers, conds = state[q]
                old = top[q]
                new = old
                for e, cond in enumerate(conds):
                    part = scores[q, e * BLOCK:(e + 1) * BLOCK, :]
                    new = jnp.maximum(new, jnp.where(cond, jnp.max(part, axis=0, keepdims=True), LOW))
                alpha = jnp.exp2((old - new) * EXP2_SCALE)
                scaled = new * EXP2_SCALE
                total = tot[q] * alpha
                for e, cond in enumerate(conds):
                    part = scores[q, e * BLOCK:(e + 1) * BLOCK, :]
                    weight = jnp.exp2(part * EXP2_SCALE - jnp.where(cond, scaled, BIG))
                    total = total + jnp.sum(weight, axis=0, keepdims=True)
                    weights[q, e * BLOCK:(e + 1) * BLOCK, :] = weight.astype(jnp.bfloat16)
                top[q] = new
                tot[q] = total
                alphas[q] = alpha
            for q in range(4):
                uppers, conds = state[q]
                vv = jnp.concatenate(
                    [jnp.where(u, kv[b0 + e, 1, BLOCK:, :], kv[b0 + e, 1, :BLOCK, :]) for e, u in enumerate(uppers)],
                    axis=0,
                )
                added = lax.dot_general(
                    vv, weights[q], (((0,), (0,)), ((), ())), preferred_element_type=jnp.float32
                )
                acc[q] = acc[q] * alphas[q] + added
            return carry

        lax.fori_loop(0, 1 + near, one_round, 0)

    def arrival(k):
        r = k // 4 + 1
        up = (k % 2 == 0).astype(jnp.int32)
        e = jnp.where(k == 13, 1, (k % 4) // 2)
        zz = (z + NZ + jnp.where(up == 1, -r, r)) % NZ
        return zz * NX + 2 * c + e, (up == 1) & (r < 4 - e), (up == 0) & (r < 3 + e)

    def step(k, carry):
        @pl.when(k < 14)
        def _():
            idx, go_up, go_down = arrival(k)
            wait_bytes(kv.at[idx], ring_recv.at[idx])
            pl.when(go_up)(lambda: ring(idx, 0))
            pl.when(go_down)(lambda: ring(idx, 1))
            to_sibling(idx)

        own_rows = pl.ds(pl.multiple_of(k * chunk, 8), chunk)
        pltpu.make_async_remote_copy(
            w_ref.at[own_rows], wbuf.at[t, own_rows], own_send, own_recv,
            device_id=(s, sibling), device_id_type=MESH,
        ).start()

        for at, event, m in W_PLAN:
            @pl.when(k == at)
            def _():
                (w_first, w_second, w_third)[event](m)

        @pl.when(k == 1)
        def _():
            for i in range(2):
                wait_bytes(qin.at[2 + i], q_recv.at[i])

        def pair(p, carry):
            pr = (p + 2) // 4
            pz = (z + NZ + jnp.where(p % 2 == 0, -pr, pr)) % NZ
            other = jnp.where((p < 2) | (p >= 14), p % 2, ((p + 2) // 2) % 2)
            pc = jnp.where(other == 1, 1 - c, c)

            @pl.when(other == 1)
            def _():
                for n in range(2):
                    slot = pz * NX + 2 * pc + n
                    wait_bytes(kv.at[slot], ring_recv.at[slot])

            compute(pz, pc)
            return carry

        first = jnp.where(k < 4, jnp.maximum(k - 1, 0), k)
        last = jnp.where(k < 3, k, k + 1)
        lax.fori_loop(first, last, pair, 0)
        return carry

    lax.fori_loop(0, 16, step, 0)
    w_third(2)
    w_third(3)

    partial = []
    for i in range(2):
        o_send[i] = acc[2 + i].astype(jnp.bfloat16)
        s_send[i, pl.ds(0, 1), :] = top[2 + i]
        s_send[i, pl.ds(1, 1), :] = tot[2 + i]
        for n, (src, dst) in enumerate(((s_send, s_recv), (o_send, o_recv))):
            copy = pltpu.make_async_remote_copy(
                src.at[i], dst.at[i], os_send.at[i, n], os_recv.at[i, n],
                device_id=(partner, t), device_id_type=MESH,
            )
            copy.start()
            partial.append(copy)
    head = y_hi * NX + x
    rows = att_buf.shape[1]
    for i in range(2):
        partial[2 * i].wait_recv()
        partial[2 * i + 1].wait_recv()
        top_one, tot_one = top[i], tot[i]
        top_two, tot_two = s_recv[i, pl.ds(0, 1), :], s_recv[i, pl.ds(1, 1), :]
        both = jnp.maximum(top_one, top_two)
        one = jnp.exp2((top_one - both) * EXP2_SCALE)
        two = jnp.exp2((top_two - both) * EXP2_SCALE)
        total = tot_one * one + tot_two * two
        merged = (acc[i] * one + o_recv[i].astype(jnp.float32) * two) / total
        att_send[i] = merged.T.astype(jnp.bfloat16)
        for other in range(4):
            src = att_send.at[i, pl.ds(other * rows, rows)]
            mine = (2 * c + i == x) & (t == other)

            @pl.when(jnp.logical_not(mine))
            def _():
                pltpu.make_async_remote_copy(
                    src, att_buf.at[head], d_send.at[i, other], d_recv.at[head],
                    device_id=(plane + 2 * c + i, other), device_id_type=MESH,
                ).start()

            @pl.when(mine)
            def _():
                pltpu.make_async_copy(src, att_buf.at[head], d_recv.at[head]).start()

    for copy in local:
        copy.wait()
    wait_bytes(wbuf.at[y_hi * 2 + 1 - c], own_recv)
    width = 512

    def project(base, columns):
        total = None
        for n in range(2):
            pair = jnp.concatenate([att_buf[base * 4 + 2 * n], att_buf[base * 4 + 2 * n + 1]], axis=1)
            term = jnp.dot(pair, wbuf[base * 2 + n, :, columns], preferred_element_type=jnp.float32)
            total = term if total is None else total + term
        return total

    for n in range(NX):
        h = y_hi * NX + n
        wait_bytes(att_buf.at[h], d_recv.at[h])

    def first_half(n, carry):
        columns = pl.ds(pl.multiple_of(n * width, width), width)
        branch[:, columns] = project(y_hi, columns)
        return carry

    lax.fori_loop(0, out_ref.shape[1] // width, first_half, 0)
    for n in range(NX):
        h = (1 - y_hi) * NX + n
        wait_bytes(att_buf.at[h], d_recv.at[h])
    wait_bytes(wbuf.at[(1 - y_hi) * 2 + 1 - c], wsib_recv)

    def second_half(n, carry):
        columns = pl.ds(pl.multiple_of(n * width, width), width)
        total = branch[:, columns] + project(1 - y_hi, columns)
        out_ref[:, columns] = (
            res[:, columns].astype(jnp.float32) + gate[:, columns] * total
        ).astype(out_ref.dtype)
        return carry

    lax.fori_loop(0, out_ref.shape[1] // width, second_half, 0)

    for jj in range(2):
        @pl.when(2 * c + jj != x)
        def _():
            for n in range(3):
                wait_bytes(qin.at[0], a_send.at[jj, n])
    for i in range(2):
        wait_bytes(qin.at[i], q_send.at[i])
    for copy in partial:
        copy.wait_send()
    for i in range(2):
        for other in range(4):
            @pl.when(jnp.logical_not((2 * c + i == x) & (t == other)))
            def _():
                wait_bytes(att_buf.at[0], d_send.at[i, other])
    wait_bytes(wbuf.at[0], own_send)
    wait_bytes(wbuf.at[0], wsib_send)
    below, above = (x + NX - 1) % NX, (x + 1) % NX
    for m in range(4):
        wait_bytes(w_piece(x, m), cross_send.at[m])
        wait_bytes(w_piece(x, m), x_send.at[0, x * 4 + m])
        wait_bytes(w_piece(x, m), x_send.at[1, x * 4 + m])
        if m % 2 == 0:
            wait_bytes(w_piece(x, m), x_send.at[0, below * 4 + m])
        else:
            wait_bytes(w_piece(x, m), x_send.at[1, above * 4 + m])

    for e in range(2):
        idx = z * NX + 2 * c + e
        for sem in (ring_send.at[0, idx], ring_send.at[1, idx], sib_send.at[idx]):
            wait_bytes(kv.at[idx], sem)

    def drain(k, carry):
        idx, go_up, go_down = arrival(k)
        wait_bytes(kv.at[idx], sib_send.at[idx])
        pl.when(go_up)(lambda: wait_bytes(kv.at[idx], ring_send.at[0, idx]))
        pl.when(go_down)(lambda: wait_bytes(kv.at[idx], ring_send.at[1, idx]))
        return carry

    lax.fori_loop(0, 14, drain, 0)


def shards(queries, keys, values, out_weight, residual, gate, block_mask):
    rows = residual.shape[0]
    toks = queries.shape[0]
    bf16, f32 = jnp.bfloat16, jnp.float32
    dma = pltpu.SemaphoreType.DMA
    width = residual.shape[1]
    return pl.pallas_call(
        attention_kernel,
        out_shape=jax.ShapeDtypeStruct((rows, width), bf16),
        in_specs=[pl.BlockSpec(memory_space=pl.ANY)] * 7,
        out_specs=pl.BlockSpec(memory_space=pltpu.VMEM),
        scratch_shapes=[
            pltpu.SMEM((2, 8, 128), jnp.int32),
            pltpu.VMEM((4, toks, HD), bf16),
            pltpu.VMEM((HALF, 2, toks, HD), bf16),
            pltpu.VMEM((4, HD, toks), f32),
            pltpu.VMEM((4, 1, toks), f32),
            pltpu.VMEM((4, 1, toks), f32),
            pltpu.VMEM((2, HD, toks), bf16),
            pltpu.VMEM((2, HD, toks), bf16),
            pltpu.VMEM((2, 8, toks), f32),
            pltpu.VMEM((2, 8, toks), f32),
            pltpu.VMEM((2, toks, HD), bf16),
            pltpu.VMEM((8, rows, HD), bf16),
            pltpu.VMEM((4, out_weight.shape[0], width), bf16),
            pltpu.VMEM((rows, width), bf16),
            pltpu.VMEM((1, width), f32),
            pltpu.VMEM((rows, width), f32),
            pltpu.VMEM((4, toks, toks), f32),
            pltpu.VMEM((4, toks, toks), bf16),
            pltpu.VMEM((4, 1, toks), f32),
            dma((2,)), dma((2, 3)), dma((2, 3)), dma((2,)), dma((2,)),
            dma((2, HALF)), dma((HALF,)), dma((HALF,)),
            dma((2, 2)), dma((2, 2)), dma((2, 4)), dma((8,)),
            dma((3,)), dma((4,)), dma((16,)), dma((2, 16)), dma, dma, dma, dma,
        ],
        compiler_params=pltpu.CompilerParams(collective_id=0, has_side_effects=True),
        name="attend",
    )(queries, keys, values, out_weight, residual, gate.reshape(1, width), block_mask)


def solution(mesh):
    return jax.shard_map(
        shards,
        mesh=mesh,
        in_specs=(
            P("seq", "tp"),
            P("seq", "tp"),
            P("seq", "tp"),
            P("tp", None),
            P(("seq", "tp"), None),
            P(),
            P(),
        ),
        out_specs=P(("seq", "tp"), None),
        check_vma=False,
    )
```

```python
import functools

import jax
import jax.numpy as jnp
from jax import lax
from jax.experimental import pallas as pl
from jax.experimental.pallas import tpu as pltpu
from jax.sharding import PartitionSpec as P

HD = 128
BLOCK = 128
LOW = -1e30
BIG = 1e30
EXP2_SCALE = 1.4426950408889634 / HD**0.5
MESH = pl.DeviceIdType.MESH

NX = 4
NZ = 8
HALF = NX * NZ


W_PLAN = (
    (2, 0, 1), (5, 0, 2), (6, 1, 0), (7, 0, 3), (8, 1, 1), (10, 2, 0), (11, 1, 2), (12, 2, 1), (14, 1, 3),
)


def div(a, b):
    return lax.div(a, jnp.int32(b))


def mod(a, b):
    return lax.rem(a, jnp.int32(b))


def wait_bytes(ref, sem):
    pltpu.make_async_copy(ref, ref, sem).wait()


def attention_kernel(
    q_ref, k_ref, v_ref, w_ref, res_ref, gate_ref, mask_ref, out_ref,
    mask_s, qin, kv, acc, top, tot, o_send, o_recv, s_send, s_recv, att_send, att_buf,
    wbuf, res, gate, branch, scores, weights, alphas,
    mask_sem, a_send, a_recv, q_send, q_recv, ring_send, ring_recv, sib_send,
    os_send, os_recv, d_send, d_recv,
    local_sem, cross_send, w_recv, x_send, wsib_send, wsib_recv, own_send, own_recv,
):
    s = lax.axis_index("seq")
    t = lax.axis_index("tp")
    y_lo = div(s, HALF)
    z = mod(div(s, NX), NZ)
    x = mod(s, NX)
    y_hi = div(t, 2)
    c = mod(t, 2)
    plane = y_lo * HALF + z * NX
    z_up = y_lo * HALF + mod(z + 1, NZ) * NX + x
    z_down = y_lo * HALF + mod(z + NZ - 1, NZ) * NX + x
    partner = (1 - y_lo) * HALF + z * NX + x
    x_up = plane + mod(x + 1, NX)
    x_down = plane + mod(x + NX - 1, NX)
    sibling = y_hi * 2 + 1 - c
    facing = (1 - y_hi) * 2 + c

    barrier = pltpu.get_barrier_semaphore()
    member = y_hi * 8 + x * 2 + c

    def greet(o, carry):
        m = mod(member + o, 16)
        pl.semaphore_signal(
            barrier, inc=1, device_id=(plane + mod(div(m, 2), 4), div(m, 8) * 2 + mod(m, 2)), device_id_type=MESH
        )
        return carry

    lax.fori_loop(1, 16, greet, 0)
    for other in (z_up, z_down, partner):
        pl.semaphore_signal(barrier, inc=1, device_id=(other, t), device_id_type=MESH)
    pl.semaphore_signal(barrier, inc=1, device_id=(partner, facing), device_id_type=MESH)

    mask_copies = []
    for n, half in enumerate((y_lo, 1 - y_lo)):
        rows = pl.ds(pl.multiple_of((half * NZ + z) * 8, 8), 8)
        copy = pltpu.make_async_copy(mask_ref.at[rows], mask_s.at[n], mask_sem.at[n])
        copy.start()
        mask_copies.append(copy)
    top[...] = jnp.full(top.shape, LOW, jnp.float32)
    tot[...] = jnp.zeros(tot.shape, jnp.float32)
    acc[...] = jnp.zeros(acc.shape, jnp.float32)
    local = []
    for n, (src, dst) in enumerate(((w_ref, wbuf.at[t]), (res_ref, res), (gate_ref, gate))):
        copy = pltpu.make_async_copy(src, dst, local_sem.at[n])
        copy.start()
        local.append(copy)
    pl.semaphore_wait(barrier, 19)

    my_slot = z * NX + x
    pieces = ((k_ref, kv.at[my_slot, 0]), (v_ref, kv.at[my_slot, 1]), (q_ref, qin.at[mod(x, 2)]))
    for jj, n in ((0, 0), (1, 0), (0, 1), (1, 1), (0, 2), (1, 2)):
        j = 2 * c + jj
        src, dst = pieces[n]
        columns = pl.ds(jj * HD, HD)

        @pl.when(j != x)
        def _():
            pltpu.make_async_remote_copy(
                src.at[:, columns], dst, a_send.at[jj, n], a_recv.at[mod(x, 2), n],
                device_id=(plane + j, y_hi * 2 + div(x, 2)), device_id_type=MESH,
            ).start()

        @pl.when(j == x)
        def _():
            pltpu.make_async_copy(src.at[:, columns], dst, a_recv.at[mod(x, 2), n]).start()

    quarter = w_ref.shape[0] // NX
    chunk = quarter // 4

    def chunk_rows(qx, m):
        return pl.ds(pl.multiple_of(qx * quarter + m * chunk, 8), chunk)

    for m in range(4):
        pltpu.make_async_remote_copy(
            w_ref.at[chunk_rows(x, m)], wbuf.at[t, chunk_rows(x, m)], cross_send.at[m], w_recv.at[x * 4 + m],
            device_id=(partner, facing), device_id_type=MESH,
        ).start()

    def w_piece(qx, m):
        return wbuf.at[facing, chunk_rows(qx, m)]

    def w_to(qx, m, direction):
        piece = w_piece(qx, m)
        pltpu.make_async_remote_copy(
            piece, piece, x_send.at[direction, qx * 4 + m], w_recv.at[qx * 4 + m],
            device_id=(x_up if direction == 0 else x_down, t), device_id_type=MESH,
        ).start()

    def w_sibling(qx, m):
        piece = w_piece(qx, m)
        pltpu.make_async_remote_copy(
            piece, piece, wsib_send, wsib_recv, device_id=(s, sibling), device_id_type=MESH
        ).start()

    def w_first(m):
        wait_bytes(w_piece(x, m), w_recv.at[x * 4 + m])
        w_to(x, m, 0)
        w_to(x, m, 1)
        w_sibling(x, m)

    def w_second(m):
        below, above = mod(x + NX - 1, NX), mod(x + 1, NX)
        wait_bytes(w_piece(below, m), w_recv.at[below * 4 + m])
        if m % 2 == 0:
            w_to(below, m, 0)
        w_sibling(below, m)
        wait_bytes(w_piece(above, m), w_recv.at[above * 4 + m])
        if m % 2 == 1:
            w_to(above, m, 1)
        w_sibling(above, m)

    def w_third(m):
        far = mod(x + 2, NX)
        wait_bytes(w_piece(far, m), w_recv.at[far * 4 + m])
        w_sibling(far, m)

    def ring(idx, direction):
        pltpu.make_async_remote_copy(
            kv.at[idx], kv.at[idx], ring_send.at[direction, idx], ring_recv.at[idx],
            device_id=(z_up if direction == 0 else z_down, t), device_id_type=MESH,
        ).start()

    def to_sibling(idx):
        pltpu.make_async_remote_copy(
            kv.at[idx], kv.at[idx], sib_send.at[idx], ring_recv.at[idx],
            device_id=(s, sibling), device_id_type=MESH,
        ).start()

    for n in range(2):
        for e in range(2):
            idx = z * NX + 2 * c + e
            piece = kv.at[idx, n]
            wait_bytes(piece, a_recv.at[e, n])
            for goal, sem in (
                ((z_up, t), ring_send.at[0, idx]), ((z_down, t), ring_send.at[1, idx]),
                ((s, sibling), sib_send.at[idx]),
            ):
                pltpu.make_async_remote_copy(
                    piece, piece, sem, ring_recv.at[idx], device_id=goal, device_id_type=MESH
                ).start()
    for i in range(2):
        wait_bytes(qin.at[i], a_recv.at[i, 2])
        pltpu.make_async_remote_copy(
            qin.at[i], qin.at[2 + i], q_send.at[i], q_recv.at[i],
            device_id=(partner, t), device_id_type=MESH,
        ).start()
    for copy in mask_copies:
        copy.wait()
    w_first(0)

    lane = lax.broadcasted_iota(jnp.int32, (1, 2 * BLOCK), 1)

    def compute(zz, cc):
        b0 = zz * NX + 2 * cc
        g0 = y_lo * HALF + b0
        near = jnp.int32(0)
        for grp, half in enumerate((y_lo, 1 - y_lo)):
            for i in range(2):
                a = half * HALF + z * NX + 2 * c + i
                for e in range(2):
                    gap = a - (g0 + e)
                    near = near | ((gap <= 2) & (gap >= -2)).astype(jnp.int32)

        def one_round(rr, carry):
            state = []
            for q in range(4):
                grp, i = q // 2, q % 2
                row = (2 * c + i) * 2
                halves_k, uppers, conds = [], [], []
                for e in range(2):
                    col = 2 * (g0 + e)
                    m00 = mask_s[grp, row, col]
                    m10 = mask_s[grp, row + 1, col]
                    m01 = mask_s[grp, row, col + 1]
                    m11 = mask_s[grp, row + 1, col + 1]
                    upper = ((m01 | m11) ^ rr) != 0
                    conds.append((jnp.where(upper, m01, m00), jnp.where(upper, m11, m10)))
                    uppers.append(upper)
                    halves_k.append(jnp.where(upper, kv[b0 + e, 0, BLOCK:, :], kv[b0 + e, 0, :BLOCK, :]))
                scores[q] = lax.dot_general(
                    jnp.concatenate(halves_k, axis=0), qin[q], (((1,), (1,)), ((), ())),
                    preferred_element_type=jnp.float32,
                )
                state.append((uppers, [jnp.where(lane < BLOCK, *pair) != 0 for pair in conds]))
            for q in range(4):
                uppers, conds = state[q]
                old = top[q]
                new = old
                for e, cond in enumerate(conds):
                    part = scores[q, e * BLOCK:(e + 1) * BLOCK, :]
                    new = jnp.maximum(new, jnp.where(cond, jnp.max(part, axis=0, keepdims=True), LOW))
                alpha = jnp.exp2((old - new) * EXP2_SCALE)
                scaled = new * EXP2_SCALE
                total = tot[q] * alpha
                for e, cond in enumerate(conds):
                    part = scores[q, e * BLOCK:(e + 1) * BLOCK, :]
                    weight = jnp.exp2(part * EXP2_SCALE - jnp.where(cond, scaled, BIG))
                    total = total + jnp.sum(weight, axis=0, keepdims=True)
                    weights[q, e * BLOCK:(e + 1) * BLOCK, :] = weight.astype(jnp.bfloat16)
                top[q] = new
                tot[q] = total
                alphas[q] = alpha
            for q in range(4):
                uppers, conds = state[q]
                vv = jnp.concatenate(
                    [jnp.where(u, kv[b0 + e, 1, BLOCK:, :], kv[b0 + e, 1, :BLOCK, :]) for e, u in enumerate(uppers)],
                    axis=0,
                )
                added = lax.dot_general(
                    vv, weights[q], (((0,), (0,)), ((), ())), preferred_element_type=jnp.float32
                )
                acc[q] = acc[q] * alphas[q] + added
            return carry

        lax.fori_loop(0, 1 + near, one_round, 0)

    def arrival(k):
        r = div(k, 4) + 1
        up = 1 - mod(k, 2)
        e = jnp.where(k == 13, 1, div(mod(k, 4), 2))
        zz = mod(z + NZ + jnp.where(up == 1, -r, r), NZ)
        return zz * NX + 2 * c + e, (up == 1) & (r < 4 - e), (up == 0) & (r < 3 + e)

    def step(k, carry):
        @pl.when(k < 14)
        def _():
            idx, go_up, go_down = arrival(k)
            wait_bytes(kv.at[idx], ring_recv.at[idx])
            pl.when(go_up)(lambda: ring(idx, 0))
            pl.when(go_down)(lambda: ring(idx, 1))
            to_sibling(idx)

        own_rows = pl.ds(pl.multiple_of(k * chunk, 8), chunk)
        pltpu.make_async_remote_copy(
            w_ref.at[own_rows], wbuf.at[t, own_rows], own_send, own_recv,
            device_id=(s, sibling), device_id_type=MESH,
        ).start()

        for at, event, m in W_PLAN:
            @pl.when(k == at)
            def _():
                (w_first, w_second, w_third)[event](m)

        @pl.when(k == 1)
        def _():
            for i in range(2):
                wait_bytes(qin.at[2 + i], q_recv.at[i])

        def pair(p, carry):
            pr = div(p + 2, 4)
            pz = mod(z + NZ + jnp.where(mod(p, 2) == 0, -pr, pr), NZ)
            other = mod(jnp.where((p < 2) | (p >= 14), p, div(p + 2, 2)), 2)
            pc = jnp.where(other == 1, 1 - c, c)

            @pl.when(other == 1)
            def _():
                for n in range(2):
                    slot = pz * NX + 2 * pc + n
                    wait_bytes(kv.at[slot], ring_recv.at[slot])

            compute(pz, pc)
            return carry

        first = jnp.where(k < 4, jnp.maximum(k - 1, 0), k)
        last = jnp.where(k < 3, k, k + 1)
        lax.fori_loop(first, last, pair, 0)
        return carry

    lax.fori_loop(0, 16, step, 0)
    partial = []
    for i in range(2):
        o_send[i] = acc[2 + i].astype(jnp.bfloat16)
        s_send[i, pl.ds(0, 1), :] = top[2 + i]
        s_send[i, pl.ds(1, 1), :] = tot[2 + i]
        for n, (src, dst) in enumerate(((s_send, s_recv), (o_send, o_recv))):
            copy = pltpu.make_async_remote_copy(
                src.at[i], dst.at[i], os_send.at[i, n], os_recv.at[i, n],
                device_id=(partner, t), device_id_type=MESH,
            )
            copy.start()
            partial.append(copy)
    w_third(2)
    head = y_hi * NX + x
    rows = att_buf.shape[1]
    for i in range(2):
        partial[2 * i].wait_recv()
        partial[2 * i + 1].wait_recv()
        top_one, tot_one = top[i], tot[i]
        top_two, tot_two = s_recv[i, pl.ds(0, 1), :], s_recv[i, pl.ds(1, 1), :]
        both = jnp.maximum(top_one, top_two)
        one = jnp.exp2((top_one - both) * EXP2_SCALE)
        two = jnp.exp2((top_two - both) * EXP2_SCALE)
        total = tot_one * one + tot_two * two
        merged = (acc[i] * one + o_recv[i].astype(jnp.float32) * two) / total
        att_send[i] = merged.T.astype(jnp.bfloat16)
        for other in range(4):
            src = att_send.at[i, pl.ds(other * rows, rows)]
            mine = (2 * c + i == x) & (t == other)

            @pl.when(jnp.logical_not(mine))
            def _():
                pltpu.make_async_remote_copy(
                    src, att_buf.at[head], d_send.at[i, other], d_recv.at[head],
                    device_id=(plane + 2 * c + i, other), device_id_type=MESH,
                ).start()

            @pl.when(mine)
            def _():
                pltpu.make_async_copy(src, att_buf.at[head], d_recv.at[head]).start()

    w_third(3)
    for jj in range(2):
        @pl.when(2 * c + jj != x)
        def _():
            for n in range(3):
                wait_bytes(qin.at[0], a_send.at[jj, n])
    for i in range(2):
        wait_bytes(qin.at[i], q_send.at[i])
    for copy in partial:
        copy.wait_send()
    wait_bytes(wbuf.at[0], own_send)
    wait_bytes(wbuf.at[0], wsib_send)
    below, above = mod(x + NX - 1, NX), mod(x + 1, NX)
    for m in range(4):
        wait_bytes(w_piece(x, m), cross_send.at[m])
        wait_bytes(w_piece(x, m), x_send.at[0, x * 4 + m])
        wait_bytes(w_piece(x, m), x_send.at[1, x * 4 + m])
        if m % 2 == 0:
            wait_bytes(w_piece(x, m), x_send.at[0, below * 4 + m])
        else:
            wait_bytes(w_piece(x, m), x_send.at[1, above * 4 + m])

    for e in range(2):
        idx = z * NX + 2 * c + e
        for sem in (ring_send.at[0, idx], ring_send.at[1, idx], sib_send.at[idx]):
            wait_bytes(kv.at[idx], sem)

    def drain(k, carry):
        idx, go_up, go_down = arrival(k)
        wait_bytes(kv.at[idx], sib_send.at[idx])
        pl.when(go_up)(lambda: wait_bytes(kv.at[idx], ring_send.at[0, idx]))
        pl.when(go_down)(lambda: wait_bytes(kv.at[idx], ring_send.at[1, idx]))
        return carry

    lax.fori_loop(0, 14, drain, 0)

    for copy in local:
        copy.wait()
    wait_bytes(wbuf.at[y_hi * 2 + 1 - c], own_recv)
    width = 512

    def project(base, columns):
        total = None
        for n in range(2):
            pair = jnp.concatenate([att_buf[base * 4 + 2 * n], att_buf[base * 4 + 2 * n + 1]], axis=1)
            term = jnp.dot(pair, wbuf[base * 2 + n, :, columns], preferred_element_type=jnp.float32)
            total = term if total is None else total + term
        return total

    for n in range(NX):
        h = y_hi * NX + n
        wait_bytes(att_buf.at[h], d_recv.at[h])

    def first_half(n, carry):
        columns = pl.ds(pl.multiple_of(n * width, width), width)
        branch[:, columns] = project(y_hi, columns)
        return carry

    lax.fori_loop(0, out_ref.shape[1] // width, first_half, 0)
    for n in range(NX):
        h = (1 - y_hi) * NX + n
        wait_bytes(att_buf.at[h], d_recv.at[h])
    wait_bytes(wbuf.at[(1 - y_hi) * 2 + 1 - c], wsib_recv)

    def second_half(n, carry):
        columns = pl.ds(pl.multiple_of(n * width, width), width)
        total = branch[:, columns] + project(1 - y_hi, columns)
        out_ref[:, columns] = (
            res[:, columns].astype(jnp.float32) + gate[:, columns] * total
        ).astype(out_ref.dtype)
        return carry

    lax.fori_loop(0, out_ref.shape[1] // width, second_half, 0)

    for i in range(2):
        for other in range(4):
            @pl.when(jnp.logical_not((2 * c + i == x) & (t == other)))
            def _():
                wait_bytes(att_buf.at[0], d_send.at[i, other])


def shards(queries, keys, values, out_weight, residual, gate, block_mask):
    rows = residual.shape[0]
    toks = queries.shape[0]
    bf16, f32 = jnp.bfloat16, jnp.float32
    dma = pltpu.SemaphoreType.DMA
    width = residual.shape[1]
    return pl.pallas_call(
        attention_kernel,
        out_shape=pltpu.VMEM((rows, width), bf16),
        in_specs=[pl.BlockSpec(memory_space=pl.ANY)] * 7,
        out_specs=pl.BlockSpec(memory_space=pltpu.VMEM),
        scratch_shapes=[
            pltpu.SMEM((2, 8, 128), jnp.int32),
            pltpu.VMEM((4, toks, HD), bf16),
            pltpu.VMEM((HALF, 2, toks, HD), bf16),
            pltpu.VMEM((4, HD, toks), f32),
            pltpu.VMEM((4, 1, toks), f32),
            pltpu.VMEM((4, 1, toks), f32),
            pltpu.VMEM((2, HD, toks), bf16),
            pltpu.VMEM((2, HD, toks), bf16),
            pltpu.VMEM((2, 8, toks), f32),
            pltpu.VMEM((2, 8, toks), f32),
            pltpu.VMEM((2, toks, HD), bf16),
            pltpu.VMEM((8, rows, HD), bf16),
            pltpu.VMEM((4, out_weight.shape[0], width), bf16),
            pltpu.VMEM((rows, width), bf16),
            pltpu.VMEM((1, width), f32),
            pltpu.VMEM((rows, width), f32),
            pltpu.VMEM((4, toks, toks), f32),
            pltpu.VMEM((4, toks, toks), bf16),
            pltpu.VMEM((4, 1, toks), f32),
            dma((2,)), dma((2, 3)), dma((2, 3)), dma((2,)), dma((2,)),
            dma((2, HALF)), dma((HALF,)), dma((HALF,)),
            dma((2, 2)), dma((2, 2)), dma((2, 4)), dma((8,)),
            dma((3,)), dma((4,)), dma((16,)), dma((2, 16)), dma, dma, dma, dma,
        ],
        compiler_params=pltpu.CompilerParams(collective_id=0, has_side_effects=True),
        name="attend",
    )(queries, keys, values, out_weight, residual, gate.reshape(1, width), block_mask)


def solution(mesh):
    return jax.shard_map(
        shards,
        mesh=mesh,
        in_specs=(
            P("seq", "tp"),
            P("seq", "tp"),
            P("seq", "tp"),
            P("tp", None),
            P(("seq", "tp"), None),
            P(),
            P(),
        ),
        out_specs=P(("seq", "tp"), None),
        check_vma=False,
    )
```

```python
import functools

import jax
import jax.numpy as jnp
from jax import lax
from jax.experimental import pallas as pl
from jax.experimental.pallas import tpu as pltpu
from jax.sharding import PartitionSpec as P

HD = 128
BLOCK = 128
LOW = -1e30
BIG = 1e30
EXP2_SCALE = 1.4426950408889634 / HD**0.5
MESH = pl.DeviceIdType.MESH

NX = 4
NZ = 8
HALF = NX * NZ


W_PLAN = (
    (2, 0, 1), (5, 0, 2), (6, 1, 0), (7, 0, 3), (8, 1, 1), (10, 2, 0), (11, 1, 2), (12, 2, 1),
)


def div(a, b):
    return lax.div(a, jnp.int32(b))


def mod(a, b):
    return lax.rem(a, jnp.int32(b))


def wait_bytes(ref, sem):
    pltpu.make_async_copy(ref, ref, sem).wait()


def attention_kernel(
    q_ref, k_ref, v_ref, w_ref, res_ref, gate_ref, mask_ref, out_ref,
    mask_s, qin, kv, acc, top, tot, o_send, o_recv, s_send, s_recv, att_send, att_buf,
    wbuf, res, gate, branch, scores, weights, alphas,
    mask_sem, a_send, a_recv, q_send, q_recv, ring_send, ring_recv, sib_send,
    os_send, os_recv, d_send, d_recv,
    local_sem, cross_send, w_recv, x_send, wsib_send, wsib_recv, own_send, own_recv,
):
    s = lax.axis_index("seq")
    t = lax.axis_index("tp")
    y_lo = div(s, HALF)
    z = mod(div(s, NX), NZ)
    x = mod(s, NX)
    y_hi = div(t, 2)
    c = mod(t, 2)
    plane = y_lo * HALF + z * NX
    z_up = y_lo * HALF + mod(z + 1, NZ) * NX + x
    z_down = y_lo * HALF + mod(z + NZ - 1, NZ) * NX + x
    partner = (1 - y_lo) * HALF + z * NX + x
    x_up = plane + mod(x + 1, NX)
    x_down = plane + mod(x + NX - 1, NX)
    sibling = y_hi * 2 + 1 - c
    facing = (1 - y_hi) * 2 + c

    barrier = pltpu.get_barrier_semaphore()
    columns_x = [plane + mod(x + n, NX) for n in range(NX)]
    chips_t = (y_hi * 2, (1 - y_hi) * 2)
    for far_hi in (1, 0):
        for dx in (2, 1, 3, 0):
            for core in (1 - c, c):
                if far_hi or dx or core is not c:
                    pl.semaphore_signal(
                        barrier, inc=1, device_id=(columns_x[dx], chips_t[far_hi] + core), device_id_type=MESH
                    )
    for other in (z_up, z_down, partner):
        pl.semaphore_signal(barrier, inc=1, device_id=(other, t), device_id_type=MESH)
    pl.semaphore_signal(barrier, inc=1, device_id=(partner, facing), device_id_type=MESH)

    mask_copies = []
    for n, half in enumerate((y_lo, 1 - y_lo)):
        rows = pl.ds(pl.multiple_of((half * NZ + z) * 8, 8), 8)
        copy = pltpu.make_async_copy(mask_ref.at[rows], mask_s.at[n], mask_sem.at[n])
        copy.start()
        mask_copies.append(copy)
    top[...] = jnp.full(top.shape, LOW, jnp.float32)
    tot[...] = jnp.zeros(tot.shape, jnp.float32)
    acc[...] = jnp.zeros(acc.shape, jnp.float32)
    local = []
    for n, (src, dst) in enumerate(((w_ref, wbuf.at[t]), (res_ref, res), (gate_ref, gate))):
        copy = pltpu.make_async_copy(src, dst, local_sem.at[n])
        copy.start()
        local.append(copy)
    pl.semaphore_wait(barrier, 19)

    my_slot = z * NX + x
    pieces = ((k_ref, kv.at[my_slot, 0]), (v_ref, kv.at[my_slot, 1]), (q_ref, qin.at[mod(x, 2)]))
    for jj, n in ((0, 0), (1, 0), (0, 1), (1, 1), (0, 2), (1, 2)):
        j = 2 * c + jj
        src, dst = pieces[n]
        columns = pl.ds(jj * HD, HD)

        @pl.when(j != x)
        def _():
            pltpu.make_async_remote_copy(
                src.at[:, columns], dst, a_send.at[jj, n], a_recv.at[mod(x, 2), n],
                device_id=(plane + j, y_hi * 2 + div(x, 2)), device_id_type=MESH,
            ).start()

        @pl.when(j == x)
        def _():
            pltpu.make_async_copy(src.at[:, columns], dst, a_recv.at[mod(x, 2), n]).start()

    quarter = w_ref.shape[0] // NX
    chunk = quarter // 4

    def chunk_rows(qx, m):
        return pl.ds(pl.multiple_of(qx * quarter + m * chunk, 8), chunk)

    for m in range(4):
        pltpu.make_async_remote_copy(
            w_ref.at[chunk_rows(x, m)], wbuf.at[t, chunk_rows(x, m)], cross_send.at[m], w_recv.at[x * 4 + m],
            device_id=(partner, facing), device_id_type=MESH,
        ).start()

    def w_piece(qx, m):
        return wbuf.at[facing, chunk_rows(qx, m)]

    def w_to(qx, m, direction):
        piece = w_piece(qx, m)
        pltpu.make_async_remote_copy(
            piece, piece, x_send.at[direction, qx * 4 + m], w_recv.at[qx * 4 + m],
            device_id=(x_up if direction == 0 else x_down, t), device_id_type=MESH,
        ).start()

    def w_sibling(qx, m):
        piece = w_piece(qx, m)
        pltpu.make_async_remote_copy(
            piece, piece, wsib_send, wsib_recv, device_id=(s, sibling), device_id_type=MESH
        ).start()

    def w_first(m):
        wait_bytes(w_piece(x, m), w_recv.at[x * 4 + m])
        w_to(x, m, 0)
        w_to(x, m, 1)
        w_sibling(x, m)

    def w_second(m):
        below, above = mod(x + NX - 1, NX), mod(x + 1, NX)
        wait_bytes(w_piece(below, m), w_recv.at[below * 4 + m])
        if m % 2 == 0:
            w_to(below, m, 0)
        w_sibling(below, m)
        wait_bytes(w_piece(above, m), w_recv.at[above * 4 + m])
        if m % 2 == 1:
            w_to(above, m, 1)
        w_sibling(above, m)

    def w_third(m):
        far = mod(x + 2, NX)
        wait_bytes(w_piece(far, m), w_recv.at[far * 4 + m])
        w_sibling(far, m)

    def ring(idx, direction):
        pltpu.make_async_remote_copy(
            kv.at[idx], kv.at[idx], ring_send.at[direction, idx], ring_recv.at[idx],
            device_id=(z_up if direction == 0 else z_down, t), device_id_type=MESH,
        ).start()

    def to_sibling(idx):
        pltpu.make_async_remote_copy(
            kv.at[idx], kv.at[idx], sib_send.at[idx], ring_recv.at[idx],
            device_id=(s, sibling), device_id_type=MESH,
        ).start()

    def launch(e, n):
        e = mod(x + e, 2)
        idx = z * NX + 2 * c + e
        piece = kv.at[idx, n]
        wait_bytes(piece, a_recv.at[e, n])
        for goal, sem in (
            ((z_up, t), ring_send.at[0, idx]), ((z_down, t), ring_send.at[1, idx]),
            ((s, sibling), sib_send.at[idx]),
        ):
            pltpu.make_async_remote_copy(
                piece, piece, sem, ring_recv.at[idx], device_id=goal, device_id_type=MESH
            ).start()

    at_home = div(x, 2) == c
    launch(0, 0)
    pl.when(at_home)(lambda: launch(0, 1))
    launch(1, 0)
    pl.when(jnp.logical_not(at_home))(lambda: launch(0, 1))
    launch(1, 1)
    for i in range(2):
        wait_bytes(qin.at[i], a_recv.at[i, 2])
        pltpu.make_async_remote_copy(
            qin.at[i], qin.at[2 + i], q_send.at[i], q_recv.at[i],
            device_id=(partner, t), device_id_type=MESH,
        ).start()
    for copy in mask_copies:
        copy.wait()
    w_first(0)

    lane = lax.broadcasted_iota(jnp.int32, (1, 2 * BLOCK), 1)

    def compute(zz, cc):
        b0 = zz * NX + 2 * cc
        g0 = y_lo * HALF + b0
        near = jnp.int32(0)
        for grp, half in enumerate((y_lo, 1 - y_lo)):
            for i in range(2):
                a = half * HALF + z * NX + 2 * c + i
                for e in range(2):
                    gap = a - (g0 + e)
                    near = near | ((gap <= 2) & (gap >= -2)).astype(jnp.int32)

        def one_round(rr, carry):
            state = []
            for q in range(4):
                grp, i = q // 2, q % 2
                row = (2 * c + i) * 2
                halves_k, uppers, conds = [], [], []
                for e in range(2):
                    col = 2 * (g0 + e)
                    m00 = mask_s[grp, row, col]
                    m10 = mask_s[grp, row + 1, col]
                    m01 = mask_s[grp, row, col + 1]
                    m11 = mask_s[grp, row + 1, col + 1]
                    upper = ((m01 | m11) ^ rr) != 0
                    conds.append((jnp.where(upper, m01, m00), jnp.where(upper, m11, m10)))
                    uppers.append(upper)
                    halves_k.append(jnp.where(upper, kv[b0 + e, 0, BLOCK:, :], kv[b0 + e, 0, :BLOCK, :]))
                scores[q] = lax.dot_general(
                    jnp.concatenate(halves_k, axis=0), qin[q], (((1,), (1,)), ((), ())),
                    preferred_element_type=jnp.float32,
                )
                state.append((uppers, [jnp.where(lane < BLOCK, *pair) != 0 for pair in conds]))
            for q in range(4):
                uppers, conds = state[q]
                old = top[q]
                new = old
                for e, cond in enumerate(conds):
                    part = scores[q, e * BLOCK:(e + 1) * BLOCK, :]
                    new = jnp.maximum(new, jnp.where(cond, jnp.max(part, axis=0, keepdims=True), LOW))
                alpha = jnp.exp2((old - new) * EXP2_SCALE)
                scaled = new * EXP2_SCALE
                total = tot[q] * alpha
                for e, cond in enumerate(conds):
                    part = scores[q, e * BLOCK:(e + 1) * BLOCK, :]
                    weight = jnp.exp2(part * EXP2_SCALE - jnp.where(cond, scaled, BIG))
                    total = total + jnp.sum(weight, axis=0, keepdims=True)
                    weights[q, e * BLOCK:(e + 1) * BLOCK, :] = weight.astype(jnp.bfloat16)
                top[q] = new
                tot[q] = total
                alphas[q] = alpha
            for q in range(4):
                uppers, conds = state[q]
                vv = jnp.concatenate(
                    [jnp.where(u, kv[b0 + e, 1, BLOCK:, :], kv[b0 + e, 1, :BLOCK, :]) for e, u in enumerate(uppers)],
                    axis=0,
                )
                added = lax.dot_general(
                    vv, weights[q], (((0,), (0,)), ((), ())), preferred_element_type=jnp.float32
                )
                acc[q] = acc[q] * alphas[q] + added
            return carry

        lax.fori_loop(0, 1 + near, one_round, 0)

    def arrival(k):
        r = div(k, 4) + 1
        up = 1 - mod(k, 2)
        e = jnp.where(k == 13, 1, div(mod(k, 4), 2))
        zz = mod(z + NZ + jnp.where(up == 1, -r, r), NZ)
        return zz * NX + 2 * c + mod(x + e, 2), (up == 1) & (r < 4 - e), (up == 0) & (r < 3 + e)

    def step(k, carry):
        @pl.when(k < 14)
        def _():
            idx, go_up, go_down = arrival(k)
            wait_bytes(kv.at[idx], ring_recv.at[idx])
            pl.when(go_up)(lambda: ring(idx, 0))
            pl.when(go_down)(lambda: ring(idx, 1))
            to_sibling(idx)

        own_rows = pl.ds(pl.multiple_of(k * chunk, 8), chunk)
        pltpu.make_async_remote_copy(
            w_ref.at[own_rows], wbuf.at[t, own_rows], own_send, own_recv,
            device_id=(s, sibling), device_id_type=MESH,
        ).start()

        for at, event, m in W_PLAN:
            @pl.when(k == at)
            def _():
                (w_first, w_second, w_third)[event](m)

        @pl.when(k == 1)
        def _():
            for i in range(2):
                wait_bytes(qin.at[2 + i], q_recv.at[i])

        def pair(p, carry):
            pr = div(p + 2, 4)
            pz = mod(z + NZ + jnp.where(mod(p, 2) == 0, -pr, pr), NZ)
            other = mod(jnp.where((p < 2) | (p >= 14), p, div(p + 2, 2)), 2)
            pc = jnp.where(other == 1, 1 - c, c)

            @pl.when(other == 1)
            def _():
                for n in range(2):
                    slot = pz * NX + 2 * pc + n
                    wait_bytes(kv.at[slot], ring_recv.at[slot])

            compute(pz, pc)
            return carry

        def pairs_before(k):
            ahead = ((k == 12) | (k == 13)).astype(jnp.int32)
            return jnp.where(k < 4, jnp.maximum(k - 1, 0), k + ahead)

        lax.fori_loop(pairs_before(k), pairs_before(k + 1), pair, 0)
        return carry

    lax.fori_loop(0, 16, step, 0)
    partial = []
    for i in range(2):
        o_send[i] = acc[2 + i].astype(jnp.bfloat16)
        s_send[i, pl.ds(0, 1), :] = top[2 + i]
        s_send[i, pl.ds(1, 1), :] = tot[2 + i]
        for n, (src, dst) in enumerate(((s_send, s_recv), (o_send, o_recv))):
            copy = pltpu.make_async_remote_copy(
                src.at[i], dst.at[i], os_send.at[i, n], os_recv.at[i, n],
                device_id=(partner, t), device_id_type=MESH,
            )
            copy.start()
            partial.append(copy)
    w_second(3)
    w_third(2)
    head = y_hi * NX + x
    rows = att_buf.shape[1]
    for i in range(2):
        partial[2 * i].wait_recv()
        partial[2 * i + 1].wait_recv()
        top_one, tot_one = top[i], tot[i]
        top_two, tot_two = s_recv[i, pl.ds(0, 1), :], s_recv[i, pl.ds(1, 1), :]
        both = jnp.maximum(top_one, top_two)
        one = jnp.exp2((top_one - both) * EXP2_SCALE)
        two = jnp.exp2((top_two - both) * EXP2_SCALE)
        share = 1.0 / (tot_one * one + tot_two * two)
        merged = acc[i] * (one * share) + o_recv[i].astype(jnp.float32) * (two * share)
        att_send[i] = merged.T.astype(jnp.bfloat16)
        for other in range(4):
            src = att_send.at[i, pl.ds(other * rows, rows)]
            mine = (2 * c + i == x) & (t == other)

            @pl.when(jnp.logical_not(mine))
            def _():
                pltpu.make_async_remote_copy(
                    src, att_buf.at[head], d_send.at[i, other], d_recv.at[head],
                    device_id=(plane + 2 * c + i, other), device_id_type=MESH,
                ).start()

            @pl.when(mine)
            def _():
                pltpu.make_async_copy(src, att_buf.at[head], d_recv.at[head]).start()

    w_third(3)
    for jj in range(2):
        @pl.when(2 * c + jj != x)
        def _():
            for n in range(3):
                wait_bytes(qin.at[0], a_send.at[jj, n])
    for i in range(2):
        wait_bytes(qin.at[i], q_send.at[i])
    for copy in partial:
        copy.wait_send()
    wait_bytes(wbuf.at[0], own_send)
    wait_bytes(wbuf.at[0], wsib_send)
    below, above = mod(x + NX - 1, NX), mod(x + 1, NX)
    for m in range(4):
        wait_bytes(w_piece(x, m), cross_send.at[m])
        wait_bytes(w_piece(x, m), x_send.at[0, x * 4 + m])
        wait_bytes(w_piece(x, m), x_send.at[1, x * 4 + m])
        if m % 2 == 0:
            wait_bytes(w_piece(x, m), x_send.at[0, below * 4 + m])
        else:
            wait_bytes(w_piece(x, m), x_send.at[1, above * 4 + m])

    for e in range(2):
        idx = z * NX + 2 * c + e
        for sem in (ring_send.at[0, idx], ring_send.at[1, idx], sib_send.at[idx]):
            wait_bytes(kv.at[idx], sem)

    def drain(k, carry):
        idx, go_up, go_down = arrival(k)
        wait_bytes(kv.at[idx], sib_send.at[idx])
        pl.when(go_up)(lambda: wait_bytes(kv.at[idx], ring_send.at[0, idx]))
        pl.when(go_down)(lambda: wait_bytes(kv.at[idx], ring_send.at[1, idx]))
        return carry

    lax.fori_loop(0, 14, drain, 0)

    for copy in local:
        copy.wait()
    wait_bytes(wbuf.at[y_hi * 2 + 1 - c], own_recv)
    width = 2560

    def project(base, columns):
        total = None
        for n in range(2):
            pair = jnp.concatenate([att_buf[base * 4 + 2 * n], att_buf[base * 4 + 2 * n + 1]], axis=1)
            term = jnp.dot(pair, wbuf[base * 2 + n, :, columns], preferred_element_type=jnp.float32)
            total = term if total is None else total + term
        return total

    for n in range(NX):
        h = y_hi * NX + n
        wait_bytes(att_buf.at[h], d_recv.at[h])

    def first_half(n, carry):
        columns = pl.ds(pl.multiple_of(n * width, width), width)
        branch[:, columns] = project(y_hi, columns)
        return carry

    lax.fori_loop(0, out_ref.shape[1] // width, first_half, 0)
    for n in range(NX):
        h = (1 - y_hi) * NX + n
        wait_bytes(att_buf.at[h], d_recv.at[h])
    wait_bytes(wbuf.at[(1 - y_hi) * 2 + 1 - c], wsib_recv)

    def second_half(n, carry):
        columns = pl.ds(pl.multiple_of(n * width, width), width)
        total = branch[:, columns] + project(1 - y_hi, columns)
        out_ref[:, columns] = (
            res[:, columns].astype(jnp.float32) + gate[:, columns] * total
        ).astype(out_ref.dtype)
        return carry

    lax.fori_loop(0, out_ref.shape[1] // width, second_half, 0)

    for i in range(2):
        for other in range(4):
            @pl.when(jnp.logical_not((2 * c + i == x) & (t == other)))
            def _():
                wait_bytes(att_buf.at[0], d_send.at[i, other])


def shards(queries, keys, values, out_weight, residual, gate, block_mask):
    rows = residual.shape[0]
    toks = queries.shape[0]
    bf16, f32 = jnp.bfloat16, jnp.float32
    dma = pltpu.SemaphoreType.DMA
    width = residual.shape[1]
    return pl.pallas_call(
        attention_kernel,
        out_shape=pltpu.VMEM((rows, width), bf16),
        in_specs=[pl.BlockSpec(memory_space=pl.ANY)] * 7,
        out_specs=pl.BlockSpec(memory_space=pltpu.VMEM),
        scratch_shapes=[
            pltpu.SMEM((2, 8, 128), jnp.int32),
            pltpu.VMEM((4, toks, HD), bf16),
            pltpu.VMEM((HALF, 2, toks, HD), bf16),
            pltpu.VMEM((4, HD, toks), f32),
            pltpu.VMEM((4, 1, toks), f32),
            pltpu.VMEM((4, 1, toks), f32),
            pltpu.VMEM((2, HD, toks), bf16),
            pltpu.VMEM((2, HD, toks), bf16),
            pltpu.VMEM((2, 8, toks), f32),
            pltpu.VMEM((2, 8, toks), f32),
            pltpu.VMEM((2, toks, HD), bf16),
            pltpu.VMEM((8, rows, HD), bf16),
            pltpu.VMEM((4, out_weight.shape[0], width), bf16),
            pltpu.VMEM((rows, width), bf16),
            pltpu.VMEM((1, width), f32),
            pltpu.VMEM((rows, width), f32),
            pltpu.VMEM((4, toks, toks), f32),
            pltpu.VMEM((4, toks, toks), bf16),
            pltpu.VMEM((4, 1, toks), f32),
            dma((2,)), dma((2, 3)), dma((2, 3)), dma((2,)), dma((2,)),
            dma((2, HALF)), dma((HALF,)), dma((HALF,)),
            dma((2, 2)), dma((2, 2)), dma((2, 4)), dma((8,)),
            dma((3,)), dma((4,)), dma((16,)), dma((2, 16)), dma, dma, dma, dma,
        ],
        compiler_params=pltpu.CompilerParams(collective_id=0, has_side_effects=True),
        name="attend",
    )(queries, keys, values, out_weight, residual, gate.reshape(1, width), block_mask)


def solution(mesh):
    return jax.shard_map(
        shards,
        mesh=mesh,
        in_specs=(
            P("seq", "tp"),
            P("seq", "tp"),
            P("seq", "tp"),
            P("tp", None),
            P(("seq", "tp"), None),
            P(),
            P(),
        ),
        out_specs=P(("seq", "tp"), None),
        check_vma=False,
    )
```

```python
import functools

import jax
import jax.numpy as jnp
from jax import lax
from jax.experimental import pallas as pl
from jax.experimental.pallas import tpu as pltpu
from jax.sharding import PartitionSpec as P

HD = 128
BLOCK = 128
LOW = -1e30
BIG = 1e30
EXP2_SCALE = 1.4426950408889634 / HD**0.5
MESH = pl.DeviceIdType.MESH

NX = 4
NZ = 8
HALF = NX * NZ


W_PLAN = (
    (1, 0, 1), (3, 0, 2), (5, 1, 0), (6, 0, 3), (7, 1, 1), (9, 2, 0), (9, 1, 2), (11, 2, 1), (12, 1, 3),
)


def div(a, b):
    return lax.div(a, jnp.int32(b))


def mod(a, b):
    return lax.rem(a, jnp.int32(b))


def wait_bytes(ref, sem):
    pltpu.make_async_copy(ref, ref, sem).wait()


def attention_kernel(
    q_ref, k_ref, v_ref, w_ref, res_ref, gate_ref, mask_ref, out_ref,
    mask_s, qin, kv, acc, top, tot, o_send, o_recv, s_send, s_recv, att_send, att_buf,
    wbuf, res, gate, branch, scores, weights, alphas,
    mask_sem, a_send, a_recv, q_send, q_recv, ring_send, ring_recv, sib_send,
    os_send, os_recv, d_send, d_recv,
    local_sem, cross_send, w_recv, x_send, wsib_send, wsib_recv, own_send, own_recv,
):
    s = lax.axis_index("seq")
    t = lax.axis_index("tp")
    y_lo = div(s, HALF)
    z = mod(div(s, NX), NZ)
    x = mod(s, NX)
    y_hi = div(t, 2)
    c = mod(t, 2)
    plane = y_lo * HALF + z * NX
    z_up = y_lo * HALF + mod(z + 1, NZ) * NX + x
    z_down = y_lo * HALF + mod(z + NZ - 1, NZ) * NX + x
    partner = (1 - y_lo) * HALF + z * NX + x
    x_up = plane + mod(x + 1, NX)
    x_down = plane + mod(x + NX - 1, NX)
    sibling = y_hi * 2 + 1 - c
    facing = (1 - y_hi) * 2 + c

    barrier = pltpu.get_barrier_semaphore()
    columns_x = [plane + mod(x + n, NX) for n in range(NX)]
    chips_t = (y_hi * 2, (1 - y_hi) * 2)
    for far_hi in (1, 0):
        for dx in (2, 1, 3, 0):
            for core in (1 - c, c):
                if far_hi or dx or core is not c:
                    pl.semaphore_signal(
                        barrier, inc=1, device_id=(columns_x[dx], chips_t[far_hi] + core), device_id_type=MESH
                    )
    for other in (z_up, z_down, partner):
        pl.semaphore_signal(barrier, inc=1, device_id=(other, t), device_id_type=MESH)
    pl.semaphore_signal(barrier, inc=1, device_id=(partner, facing), device_id_type=MESH)

    mask_copies = []
    for n, half in enumerate((y_lo, 1 - y_lo)):
        rows = pl.ds(pl.multiple_of((half * NZ + z) * 8, 8), 8)
        copy = pltpu.make_async_copy(mask_ref.at[rows], mask_s.at[n], mask_sem.at[n])
        copy.start()
        mask_copies.append(copy)
    top[...] = jnp.full(top.shape, LOW, jnp.float32)
    tot[...] = jnp.zeros(tot.shape, jnp.float32)
    acc[...] = jnp.zeros(acc.shape, jnp.float32)
    local = []
    for n, (src, dst) in enumerate(((w_ref, wbuf.at[t]), (res_ref, res), (gate_ref, gate))):
        copy = pltpu.make_async_copy(src, dst, local_sem.at[n])
        copy.start()
        local.append(copy)
    pl.semaphore_wait(barrier, 19)

    my_slot = z * NX + x
    pieces = ((k_ref, kv.at[my_slot, 0]), (v_ref, kv.at[my_slot, 1]), (q_ref, qin.at[mod(x, 2)]))
    for jj, n in ((0, 0), (1, 0), (0, 1), (1, 1), (0, 2), (1, 2)):
        j = 2 * c + jj
        src, dst = pieces[n]
        columns = pl.ds(jj * HD, HD)

        @pl.when(j != x)
        def _():
            pltpu.make_async_remote_copy(
                src.at[:, columns], dst, a_send.at[jj, n], a_recv.at[mod(x, 2), n],
                device_id=(plane + j, y_hi * 2 + div(x, 2)), device_id_type=MESH,
            ).start()

        @pl.when(j == x)
        def _():
            pltpu.make_async_copy(src.at[:, columns], dst, a_recv.at[mod(x, 2), n]).start()

    quarter = w_ref.shape[0] // NX
    chunk = quarter // 4

    def chunk_rows(qx, m):
        return pl.ds(pl.multiple_of(qx * quarter + m * chunk, 8), chunk)

    for m in range(4):
        pltpu.make_async_remote_copy(
            w_ref.at[chunk_rows(x, m)], wbuf.at[t, chunk_rows(x, m)], cross_send.at[m], w_recv.at[x * 4 + m],
            device_id=(partner, facing), device_id_type=MESH,
        ).start()

    def w_piece(qx, m):
        return wbuf.at[facing, chunk_rows(qx, m)]

    def w_to(qx, m, direction):
        piece = w_piece(qx, m)
        pltpu.make_async_remote_copy(
            piece, piece, x_send.at[direction, qx * 4 + m], w_recv.at[qx * 4 + m],
            device_id=(x_up if direction == 0 else x_down, t), device_id_type=MESH,
        ).start()

    def w_sibling(qx, m):
        piece = w_piece(qx, m)
        pltpu.make_async_remote_copy(
            piece, piece, wsib_send, wsib_recv, device_id=(s, sibling), device_id_type=MESH
        ).start()

    def w_first(m):
        wait_bytes(w_piece(x, m), w_recv.at[x * 4 + m])
        w_to(x, m, 0)
        w_to(x, m, 1)
        w_sibling(x, m)

    def w_second(m):
        below, above = mod(x + NX - 1, NX), mod(x + 1, NX)
        wait_bytes(w_piece(below, m), w_recv.at[below * 4 + m])
        if m % 2 == 0:
            w_to(below, m, 0)
        w_sibling(below, m)
        wait_bytes(w_piece(above, m), w_recv.at[above * 4 + m])
        if m % 2 == 1:
            w_to(above, m, 1)
        w_sibling(above, m)

    def w_third(m):
        far = mod(x + 2, NX)
        wait_bytes(w_piece(far, m), w_recv.at[far * 4 + m])
        w_sibling(far, m)

    def ring(idx, direction):
        pltpu.make_async_remote_copy(
            kv.at[idx], kv.at[idx], ring_send.at[direction, idx], ring_recv.at[idx],
            device_id=(z_up if direction == 0 else z_down, t), device_id_type=MESH,
        ).start()

    def to_sibling(idx):
        pltpu.make_async_remote_copy(
            kv.at[idx], kv.at[idx], sib_send.at[idx], ring_recv.at[idx],
            device_id=(s, sibling), device_id_type=MESH,
        ).start()

    def launch(e, n):
        e = mod(x + e, 2)
        idx = z * NX + 2 * c + e
        piece = kv.at[idx, n]
        wait_bytes(piece, a_recv.at[e, n])
        for goal, sem in (
            ((z_up, t), ring_send.at[0, idx]), ((z_down, t), ring_send.at[1, idx]),
            ((s, sibling), sib_send.at[idx]),
        ):
            pltpu.make_async_remote_copy(
                piece, piece, sem, ring_recv.at[idx], device_id=goal, device_id_type=MESH
            ).start()

    at_home = div(x, 2) == c
    launch(0, 0)
    pl.when(at_home)(lambda: launch(0, 1))
    launch(1, 0)
    pl.when(jnp.logical_not(at_home))(lambda: launch(0, 1))
    launch(1, 1)
    for i in range(2):
        wait_bytes(qin.at[i], a_recv.at[i, 2])
        pltpu.make_async_remote_copy(
            qin.at[i], qin.at[2 + i], q_send.at[i], q_recv.at[i],
            device_id=(partner, t), device_id_type=MESH,
        ).start()
    for copy in mask_copies:
        copy.wait()
    w_first(0)

    lane = lax.broadcasted_iota(jnp.int32, (1, 2 * BLOCK), 1)

    def tiles(zz, cc, rr, queries):
        b0 = zz * NX + 2 * cc
        g0 = y_lo * HALF + b0
        state = {}
        for q in queries:
            grp, i = q // 2, q % 2
            row = (2 * c + i) * 2
            halves_k, uppers, conds = [], [], []
            for e in range(2):
                col = 2 * (g0 + e)
                m00 = mask_s[grp, row, col]
                m10 = mask_s[grp, row + 1, col]
                m01 = mask_s[grp, row, col + 1]
                m11 = mask_s[grp, row + 1, col + 1]
                upper = ((m01 | m11) ^ rr) != 0
                conds.append((jnp.where(upper, m01, m00), jnp.where(upper, m11, m10)))
                uppers.append(upper)
                halves_k.append(jnp.where(upper, kv[b0 + e, 0, BLOCK:, :], kv[b0 + e, 0, :BLOCK, :]))
            scores[q] = lax.dot_general(
                jnp.concatenate(halves_k, axis=0), qin[q], (((1,), (1,)), ((), ())),
                preferred_element_type=jnp.float32,
            )
            state[q] = (uppers, [jnp.where(lane < BLOCK, *pair) != 0 for pair in conds])
        for q in queries:
            uppers, conds = state[q]
            old = top[q]
            new = old
            for e, cond in enumerate(conds):
                part = scores[q, e * BLOCK:(e + 1) * BLOCK, :]
                new = jnp.maximum(new, jnp.where(cond, jnp.max(part, axis=0, keepdims=True), LOW))
            alpha = jnp.exp2((old - new) * EXP2_SCALE)
            scaled = new * EXP2_SCALE
            total = tot[q] * alpha
            for e, cond in enumerate(conds):
                part = scores[q, e * BLOCK:(e + 1) * BLOCK, :]
                weight = jnp.exp2(part * EXP2_SCALE - jnp.where(cond, scaled, BIG))
                total = total + jnp.sum(weight, axis=0, keepdims=True)
                weights[q, e * BLOCK:(e + 1) * BLOCK, :] = weight.astype(jnp.bfloat16)
            top[q] = new
            tot[q] = total
            alphas[q] = alpha
        for q in queries:
            uppers, conds = state[q]
            vv = jnp.concatenate(
                [jnp.where(u, kv[b0 + e, 1, BLOCK:, :], kv[b0 + e, 1, :BLOCK, :]) for e, u in enumerate(uppers)],
                axis=0,
            )
            added = lax.dot_general(
                vv, weights[q], (((0,), (0,)), ((), ())), preferred_element_type=jnp.float32
            )
            acc[q] = acc[q] * alphas[q] + added

    def compute(zz, cc):
        tiles(zz, cc, 0, range(4))
        g0 = y_lo * HALF + zz * NX + 2 * cc
        for grp, half in enumerate((y_lo, 1 - y_lo)):
            gap = half * HALF + z * NX + 2 * c - g0

            @pl.when((gap <= 3) & (gap >= -3))
            def _():
                tiles(zz, cc, 1, (2 * grp, 2 * grp + 1))

    def arrival(k):
        r = div(k, 4) + 1
        up = 1 - mod(k, 2)
        e = jnp.where(k == 13, 1, div(mod(k, 4), 2))
        zz = mod(z + NZ + jnp.where(up == 1, -r, r), NZ)
        return zz * NX + 2 * c + mod(x + e, 2), (up == 1) & (r < 4 - e), (up == 0) & (r < 3 + e)

    def step(k, carry):
        @pl.when(k < 14)
        def _():
            idx, go_up, go_down = arrival(k)
            wait_bytes(kv.at[idx], ring_recv.at[idx])
            pl.when(go_up)(lambda: ring(idx, 0))
            pl.when(go_down)(lambda: ring(idx, 1))
            to_sibling(idx)

        own_rows = pl.ds(pl.multiple_of(k * chunk, 8), chunk)
        pltpu.make_async_remote_copy(
            w_ref.at[own_rows], wbuf.at[t, own_rows], own_send, own_recv,
            device_id=(s, sibling), device_id_type=MESH,
        ).start()

        for at, event, m in W_PLAN:
            @pl.when(k == at)
            def _():
                (w_first, w_second, w_third)[event](m)

        @pl.when(k == 1)
        def _():
            for i in range(2):
                wait_bytes(qin.at[2 + i], q_recv.at[i])

        def pair(p, carry):
            pr = div(p + 2, 4)
            pz = mod(z + NZ + jnp.where(mod(p, 2) == 0, -pr, pr), NZ)
            other = mod(jnp.where((p < 2) | (p >= 14), p, div(p + 2, 2)), 2)
            pc = jnp.where(other == 1, 1 - c, c)

            @pl.when(other == 1)
            def _():
                for n in range(2):
                    slot = pz * NX + 2 * pc + n
                    wait_bytes(kv.at[slot], ring_recv.at[slot])

            compute(pz, pc)
            return carry

        def pairs_before(k):
            ahead = ((k == 12) | (k == 13)).astype(jnp.int32)
            return jnp.where(k < 4, jnp.maximum(k - 1, 0), k + ahead)

        lax.fori_loop(pairs_before(k), pairs_before(k + 1), pair, 0)
        return carry

    lax.fori_loop(0, 15, step, 0)
    own_rows = pl.ds(15 * chunk, chunk)
    pltpu.make_async_remote_copy(
        w_ref.at[own_rows], wbuf.at[t, own_rows], own_send, own_recv,
        device_id=(s, sibling), device_id_type=MESH,
    ).start()
    last = mod(z + 4, NZ)
    for n in range(2):
        slot = last * NX + 2 * (1 - c) + n
        wait_bytes(kv.at[slot], ring_recv.at[slot])
    tiles(last, 1 - c, 0, (2, 3))
    partial = []
    for i in range(2):
        o_send[i] = acc[2 + i].astype(jnp.bfloat16)
        s_send[i, pl.ds(0, 1), :] = top[2 + i]
        s_send[i, pl.ds(1, 1), :] = tot[2 + i]
        for n, (src, dst) in enumerate(((s_send, s_recv), (o_send, o_recv))):
            copy = pltpu.make_async_remote_copy(
                src.at[i], dst.at[i], os_send.at[i, n], os_recv.at[i, n],
                device_id=(partner, t), device_id_type=MESH,
            )
            copy.start()
            partial.append(copy)
    tiles(last, 1 - c, 0, (0, 1))
    head = y_hi * NX + x
    rows = att_buf.shape[1]
    for i in range(2):
        partial[2 * i].wait_recv()
        partial[2 * i + 1].wait_recv()
        top_one, tot_one = top[i], tot[i]
        top_two, tot_two = s_recv[i, pl.ds(0, 1), :], s_recv[i, pl.ds(1, 1), :]
        both = jnp.maximum(top_one, top_two)
        one = jnp.exp2((top_one - both) * EXP2_SCALE)
        two = jnp.exp2((top_two - both) * EXP2_SCALE)
        share = 1.0 / (tot_one * one + tot_two * two)
        merged = acc[i] * (one * share) + o_recv[i].astype(jnp.float32) * (two * share)
        att_send[i] = merged.astype(jnp.bfloat16).T
        for other in range(4):
            src = att_send.at[i, pl.ds(other * rows, rows)]
            mine = (2 * c + i == x) & (t == other)

            @pl.when(jnp.logical_not(mine))
            def _():
                pltpu.make_async_remote_copy(
                    src, att_buf.at[head], d_send.at[i, other], d_recv.at[head],
                    device_id=(plane + 2 * c + i, other), device_id_type=MESH,
                ).start()

            @pl.when(mine)
            def _():
                pltpu.make_async_copy(src, att_buf.at[head], d_recv.at[head]).start()

    w_third(2)
    w_third(3)
    for jj in range(2):
        @pl.when(2 * c + jj != x)
        def _():
            for n in range(3):
                wait_bytes(qin.at[0], a_send.at[jj, n])
    for i in range(2):
        wait_bytes(qin.at[i], q_send.at[i])
    for copy in partial:
        copy.wait_send()
    wait_bytes(wbuf.at[0], own_send)
    wait_bytes(wbuf.at[0], wsib_send)
    below, above = mod(x + NX - 1, NX), mod(x + 1, NX)
    for m in range(4):
        wait_bytes(w_piece(x, m), cross_send.at[m])
        wait_bytes(w_piece(x, m), x_send.at[0, x * 4 + m])
        wait_bytes(w_piece(x, m), x_send.at[1, x * 4 + m])
        if m % 2 == 0:
            wait_bytes(w_piece(x, m), x_send.at[0, below * 4 + m])
        else:
            wait_bytes(w_piece(x, m), x_send.at[1, above * 4 + m])

    for e in range(2):
        idx = z * NX + 2 * c + e
        for sem in (ring_send.at[0, idx], ring_send.at[1, idx], sib_send.at[idx]):
            wait_bytes(kv.at[idx], sem)

    def drain(k, carry):
        idx, go_up, go_down = arrival(k)
        wait_bytes(kv.at[idx], sib_send.at[idx])
        pl.when(go_up)(lambda: wait_bytes(kv.at[idx], ring_send.at[0, idx]))
        pl.when(go_down)(lambda: wait_bytes(kv.at[idx], ring_send.at[1, idx]))
        return carry

    lax.fori_loop(0, 14, drain, 0)

    for copy in local:
        copy.wait()
    wait_bytes(wbuf.at[y_hi * 2 + 1 - c], own_recv)
    width = 2560

    def project(base, columns):
        total = None
        for n in range(2):
            pair = jnp.concatenate([att_buf[base * 4 + 2 * n], att_buf[base * 4 + 2 * n + 1]], axis=1)
            term = jnp.dot(pair, wbuf[base * 2 + n, :, columns], preferred_element_type=jnp.float32)
            total = term if total is None else total + term
        return total

    for n in range(NX):
        h = y_hi * NX + n
        wait_bytes(att_buf.at[h], d_recv.at[h])

    def first_half(n, carry):
        columns = pl.ds(pl.multiple_of(n * width, width), width)
        branch[:, columns] = project(y_hi, columns)
        return carry

    lax.fori_loop(0, out_ref.shape[1] // width, first_half, 0)
    for n in range(NX):
        h = (1 - y_hi) * NX + n
        wait_bytes(att_buf.at[h], d_recv.at[h])
    wait_bytes(wbuf.at[(1 - y_hi) * 2 + 1 - c], wsib_recv)

    def second_half(n, carry):
        columns = pl.ds(pl.multiple_of(n * width, width), width)
        total = branch[:, columns] + project(1 - y_hi, columns)
        out_ref[:, columns] = (
            res[:, columns].astype(jnp.float32) + gate[:, columns] * total
        ).astype(out_ref.dtype)
        return carry

    lax.fori_loop(0, out_ref.shape[1] // width, second_half, 0)

    for i in range(2):
        for other in range(4):
            @pl.when(jnp.logical_not((2 * c + i == x) & (t == other)))
            def _():
                wait_bytes(att_buf.at[0], d_send.at[i, other])


def shards(queries, keys, values, out_weight, residual, gate, block_mask):
    rows = residual.shape[0]
    toks = queries.shape[0]
    bf16, f32 = jnp.bfloat16, jnp.float32
    dma = pltpu.SemaphoreType.DMA
    width = residual.shape[1]
    return pl.pallas_call(
        attention_kernel,
        out_shape=pltpu.VMEM((rows, width), bf16),
        in_specs=[pl.BlockSpec(memory_space=pl.ANY)] * 7,
        out_specs=pl.BlockSpec(memory_space=pltpu.VMEM),
        scratch_shapes=[
            pltpu.SMEM((2, 8, 128), jnp.int32),
            pltpu.VMEM((4, toks, HD), bf16),
            pltpu.VMEM((HALF, 2, toks, HD), bf16),
            pltpu.VMEM((4, HD, toks), f32),
            pltpu.VMEM((4, 1, toks), f32),
            pltpu.VMEM((4, 1, toks), f32),
            pltpu.VMEM((2, HD, toks), bf16),
            pltpu.VMEM((2, HD, toks), bf16),
            pltpu.VMEM((2, 8, toks), f32),
            pltpu.VMEM((2, 8, toks), f32),
            pltpu.VMEM((2, toks, HD), bf16),
            pltpu.VMEM((8, rows, HD), bf16),
            pltpu.VMEM((4, out_weight.shape[0], width), bf16),
            pltpu.VMEM((rows, width), bf16),
            pltpu.VMEM((1, width), f32),
            pltpu.VMEM((rows, width), f32),
            pltpu.VMEM((4, toks, toks), f32),
            pltpu.VMEM((4, toks, toks), bf16),
            pltpu.VMEM((4, 1, toks), f32),
            dma((2,)), dma((2, 3)), dma((2, 3)), dma((2,)), dma((2,)),
            dma((2, HALF)), dma((HALF,)), dma((HALF,)),
            dma((2, 2)), dma((2, 2)), dma((2, 4)), dma((8,)),
            dma((3,)), dma((4,)), dma((16,)), dma((2, 16)), dma, dma, dma, dma,
        ],
        compiler_params=pltpu.CompilerParams(collective_id=0, has_side_effects=True),
        name="attend",
    )(queries, keys, values, out_weight, residual, gate.reshape(1, width), block_mask)


def solution(mesh):
    return jax.shard_map(
        shards,
        mesh=mesh,
        in_specs=(
            P("seq", "tp"),
            P("seq", "tp"),
            P("seq", "tp"),
            P("tp", None),
            P(("seq", "tp"), None),
            P(),
            P(),
        ),
        out_specs=P(("seq", "tp"), None),
        check_vma=False,
    )
```
